32 devices in a mesh: cx: 8 (over z, x), cy: 4 (over y, core).
Axes of the slice: x: 2, y: 2, z: 4, core: 2. Of those that a mesh axis runs over, the one named last changes fastest.
Arguments:
- cell_pos: float32 [32, 16, 3, 1024], P('cx', 'cy'), may hold values from -6 to 6
- cell_drag: float32 [32, 16], P('cx', 'cy'), may hold values from 0.2 to 2
- cell_near: int32 [32, 16, 2], P('cx', 'cy'), may hold values from 0 to 511, as said below
- analysis: bfloat16 [1024, 1024], replicated, may hold values from -0.1875 to 0.1875
- stiffness: float32 [1024], replicated, may hold values from 0.1 to 1
- synthesis: bfloat16 [1024, 1024], replicated, may hold values from -0.1875 to 0.1875
- wall_pos: float32 [256, 3, 256], P(('cx', 'cy')), may hold values from -9 to 9
- wall_normal: float32 [256, 3, 256], P(('cx', 'cy')), may hold values from -6 to 6
- wall_weight: float32 [256, 256], P(('cx', 'cy')), may hold values from 0.02 to 0.2
- density: float32 [256, 3, 256], P(('cx', 'cy')), may hold values from -6 to 6
- patch_near: int32 [256, 4], P(('cx', 'cy')), may hold values from 0 to 255, as said below
- cell_to_patch: int32 [256, 2], P(('cx', 'cy')), may hold values from 0 to 511, as said below
Outputs:
- moved_cells: float32 [32, 16, 3, 1024], P('cx', 'cy')
- density_next: float32 [256, 3, 256], P(('cx', 'cy'))
The draws below stay inside these ranges and needn't reach their ends.
Inputs may be any that keep to these rules, and one draw needn't show every extreme that they name: `cell_near`: each entry is the row-major index (row times 16 plus column) of a cell whose grid row and column differ from the listing cell's by at most 3 each, cyclically, and never the listing cell itself. `cell_to_patch`: for the patches of block b (patches b * 8 to b * 8 + 7), with b = i * 4 + j, each entry is the row-major index of a cell whose row lies within 3 of the rows i * 4 to i * 4 + 3 and whose column lies within 3 of the columns j * 4 to j * 4 + 3, cyclically. `patch_near`: each entry is a patch of the listing patch's block of 8 or of the two blocks beside it, cyclically, and never the listing patch itself.
All inputs are finite; a program needn't handle non-finite values.
Results may differ from the reference program's by a relative error of at most 0.0041.
Values sent between devices are 32-bit elements; how exact they have to be, the bound alone decides.
A program may use at most 64 MiB of HBM per device.

```python
import math
import jax
import jax.numpy as jnp
from jax import lax

P_SIZE = 1024
Q = 1024
PP = 256
HALO = 3
NEAR = 2
CPNEAR = 2
PNEAR = 4
CXD = 4
CYD = 4
PATCH_DEV = 8
NXC = 32
NYC = 16
PATCHES = 256
N_CY = 4


def draw_cell_near(key, part):
    window = 2 * HALO + 1
    centre = HALO * window + HALO
    picked = jax.random.randint(key, (NXC, NYC, NEAR), 0, window * window - 1)
    picked = picked + (picked >= centre).astype(jnp.int32)
    shift_row = picked // window - HALO
    shift_col = picked % window - HALO
    grid_row = jnp.arange(NXC, dtype=jnp.int32)[:, None, None]
    grid_col = jnp.arange(NYC, dtype=jnp.int32)[None, :, None]
    return ((grid_row + shift_row) % NXC * NYC + (grid_col + shift_col) % NYC).astype(jnp.int32)


def draw_cell_to_patch(key, part):
    first_key, second_key = jax.random.split(jax.random.fold_in(key, 7))
    patch_ids = jnp.arange(PATCHES, dtype=jnp.int32)[:, None]
    block = patch_ids // PATCH_DEV
    block_row = block // N_CY
    block_col = block % N_CY
    offset_row = jax.random.randint(first_key, (PATCHES, CPNEAR), 0, CXD + 2 * HALO)
    offset_col = jax.random.randint(second_key, (PATCHES, CPNEAR), 0, CYD + 2 * HALO)
    grid_row = (block_row * CXD - HALO + offset_row) % NXC
    grid_col = (block_col * CYD - HALO + offset_col) % NYC
    return (grid_row * NYC + grid_col).astype(jnp.int32)


def draw_patch_near(key, part):
    picked = jax.random.randint(jax.random.fold_in(key, 11), (PATCHES, PNEAR), 0, 3 * PATCH_DEV - 1)
    patch_ids = jnp.arange(PATCHES, dtype=jnp.int32)[:, None]
    itself = patch_ids % PATCH_DEV + PATCH_DEV
    picked = picked + (picked >= itself).astype(jnp.int32)
    base = patch_ids // PATCH_DEV * PATCH_DEV - PATCH_DEV
    return ((base + picked) % PATCHES).astype(jnp.int32)


def steps_of(rng, dims, shards, least, top_value):
    gain, own = 1.0, jax.random.fold_in(rng, 6)
    for position, shards_of in shards:
        heights = jnp.exp(jax.random.uniform(jax.random.fold_in(own, position), (shards_of,), jnp.float32, least / len(shards), top_value / len(shards)))
        gain = gain * jnp.repeat(heights, dims[position] // shards_of).reshape([-1 if axis == position else 1 for axis in range(len(dims))])
    return gain


def gaussian(rng, extent, deviation, most, shards=(), held_as=jnp.bfloat16):
    result = deviation * jax.random.normal(rng, extent, jnp.float32)
    if shards:
        result = result * steps_of(rng, extent, shards, -0.22, 0.18)
    return jnp.clip(result, -most, most).astype(held_as)


def setup_inputs(seed: int = 0) -> dict:
    splits = jax.random.split(jax.random.key(seed), 13)
    cell_pos = gaussian(splits[0], (NXC, NYC, 3, P_SIZE), 1.0, 6.0, ((0, 8), (1, 4)), jnp.float32)
    cell_drag = jnp.clip(jnp.exp(math.log(2.0) - 2.3025851 * jax.random.uniform(splits[1], (NXC, NYC), jnp.float32) ** steps_of(splits[1], (NXC, NYC), ((0, 8), (1, 4)), -0.2, 0.2)), 0.2, 2.0)
    cell_near = draw_cell_near(jax.random.fold_in(splits[12], 71), 0)
    analysis = gaussian(splits[3], (P_SIZE, Q), P_SIZE ** -0.5, 0.1875)
    stiffness = jnp.clip(jnp.exp(jax.random.uniform(splits[4], (Q,), jnp.float32, math.log(0.1), math.log(1.0))), 0.1, 1.0)
    synthesis = gaussian(splits[5], (Q, P_SIZE), Q ** -0.5, 0.1875)
    wall_pos = gaussian(splits[6], (PATCHES, 3, PP), 1.5, 9.0, ((0, 32),), jnp.float32)
    wall_normal = gaussian(splits[7], (PATCHES, 3, PP), 1.0, 6.0, ((0, 32),), jnp.float32)
    wall_weight = jnp.clip(jnp.exp(math.log(0.2) - 2.3025851 * jax.random.uniform(splits[8], (PATCHES, PP), jnp.float32) ** steps_of(splits[8], (PATCHES, PP), ((0, 32),), -0.2, 0.2)), 0.02, 0.2)
    density = gaussian(splits[9], (PATCHES, 3, PP), 1.0, 6.0, ((0, 32),), jnp.float32)
    patch_near = draw_patch_near(jax.random.fold_in(splits[12], 71), 0)
    cell_to_patch = draw_cell_to_patch(jax.random.fold_in(splits[12], 71), 0)
    return dict(cell_pos=cell_pos, cell_drag=cell_drag, cell_near=cell_near, analysis=analysis, stiffness=stiffness, synthesis=synthesis, wall_pos=wall_pos, wall_normal=wall_normal, wall_weight=wall_weight, density=density, patch_near=patch_near, cell_to_patch=cell_to_patch)


soften = 0.25
stokes_scale = 1.0 / (8.0 * math.pi)
layer_scale = 3.0 / (4.0 * math.pi)

def membrane(positions, analysis, stiffness, synthesis):
    points = positions.shape[-1]
    centred = positions - lax.optimization_barrier(jnp.mean(positions, axis=-1, keepdims=True))
    flat = centred.reshape(-1, points).astype(jnp.bfloat16)
    coeff = jnp.dot(flat, analysis, preferred_element_type=jnp.float32)
    scaled = (coeff * stiffness[None, :]).astype(jnp.bfloat16)
    force = -jnp.dot(scaled, synthesis, preferred_element_type=jnp.float32)
    return force.reshape(positions.shape)

def stokeslet(targets, sources, forces):
    delta_x = targets[0][:, None] - sources[0][None, :]
    delta_y = targets[1][:, None] - sources[1][None, :]
    delta_z = targets[2][:, None] - sources[2][None, :]
    square = delta_x * delta_x + delta_y * delta_y + delta_z * delta_z + soften
    factor = lax.rsqrt(square) / square
    along = delta_x * forces[0][None, :] + delta_y * forces[1][None, :] + delta_z * forces[2][None, :]
    direct = (square + soften) * factor
    tangent = along * factor
    out_x = lax.optimization_barrier(jnp.sum(direct * forces[0][None, :] + tangent * delta_x, axis=1))
    out_y = lax.optimization_barrier(jnp.sum(direct * forces[1][None, :] + tangent * delta_y, axis=1))
    out_z = lax.optimization_barrier(jnp.sum(direct * forces[2][None, :] + tangent * delta_z, axis=1))
    return stokes_scale * jnp.stack([out_x, out_y, out_z])

def double_layer(targets, sources, normals, weights, values):
    delta_x = targets[0][:, None] - sources[0][None, :]
    delta_y = targets[1][:, None] - sources[1][None, :]
    delta_z = targets[2][:, None] - sources[2][None, :]
    square = delta_x * delta_x + delta_y * delta_y + delta_z * delta_z + soften
    factor = lax.rsqrt(square) / (square * square)
    along_q = delta_x * values[0][None, :] + delta_y * values[1][None, :] + delta_z * values[2][None, :]
    along_n = delta_x * normals[0][None, :] + delta_y * normals[1][None, :] + delta_z * normals[2][None, :]
    scalar = -layer_scale * weights[None, :] * along_q * along_n * factor
    return jnp.stack([lax.optimization_barrier(jnp.sum(scalar * delta_x, axis=1)), lax.optimization_barrier(jnp.sum(scalar * delta_y, axis=1)), lax.optimization_barrier(jnp.sum(scalar * delta_z, axis=1))])

def spread(picked):
    count = picked.shape[0]
    return jnp.swapaxes(picked, 0, 1).reshape(3, count * picked.shape[-1])

def reference(cell_pos, cell_drag, cell_near, analysis, stiffness, synthesis, wall_pos, wall_normal, wall_weight, density, patch_near, cell_to_patch):
    forces = membrane(cell_pos, analysis, stiffness, synthesis)
    flat_pos = cell_pos.reshape(NXC * NYC, 3, P_SIZE)
    flat_force = forces.reshape(NXC * NYC, 3, P_SIZE)

    def one_cell(target, neighbours):
        return stokeslet(target, spread(flat_pos[neighbours]), spread(flat_force[neighbours]))

    def one_row(pieces):
        return jax.vmap(one_cell)(pieces[0], pieces[1])
    near = lax.map(one_row, (cell_pos, cell_near))
    velocity = cell_drag[:, :, None, None] * forces + near
    speed = jnp.sqrt(lax.optimization_barrier(jnp.sum(velocity * velocity, axis=2)))
    step = 1.0 / (jnp.max(speed) + 1e-06)
    moved_cells = cell_pos + step * velocity

    def wall_from_cells(pieces):
        target, listed = pieces
        return stokeslet(target, spread(flat_pos[listed]), spread(flat_force[listed]))
    wall_velocity = lax.map(wall_from_cells, (wall_pos, cell_to_patch))
    patch_ids = jnp.arange(PATCHES, dtype=jnp.int32)

    def layer_patch(pieces):
        own, target, listed = pieces
        chosen = jnp.concatenate([own[None], listed]).astype(jnp.int32)
        return double_layer(target, spread(wall_pos[chosen]), spread(wall_normal[chosen]), wall_weight[chosen].reshape(-1), spread(density[chosen]))
    layer = lax.map(layer_patch, (patch_ids, wall_pos, patch_near))
    density_next = 2.0 * layer + 2.0 * wall_velocity
    return (moved_cells, density_next)
```

```python
import functools
import math

import jax
import jax.numpy as jnp
from jax import lax
from jax.experimental import pallas as pl
from jax.experimental.pallas import tpu as pltpu
from jax.sharding import PartitionSpec as P

HALO = 3
LANES = 128
WIDTH = 512

soften = 0.25
stokes_scale = 1.0 / (8.0 * math.pi)
layer_scale = 3.0 / (4.0 * math.pi)

MESH = pl.DeviceIdType.MESH
f32 = jnp.float32
bf16 = jnp.bfloat16


def pieces(value):
    high = value.astype(bf16).astype(f32)
    rest = value - high
    middle = rest.astype(bf16).astype(f32)
    return high, middle, rest - middle


def strided(ref, start, count, stride):
    return ref[pl.ds(start, count, stride=stride), :]


def put_wide(ref, first, value):
    tiles = value.shape[1] // LANES
    height = ref.shape[0] // tiles
    for k in range(tiles):
        at = k * height + first
        ref[at : at + value.shape[0], :] = value[:, k * LANES : (k + 1) * LANES]


def get_tile(ref, tiles, tile, start, count, stride):
    height = ref.shape[0] // tiles
    return ref[pl.ds(tile * height + start, count, stride=stride), :]


def get_wide(ref, tiles, start, count, stride):
    return jnp.concatenate([get_tile(ref, tiles, k, start, count, stride) for k in range(tiles)], axis=1)


class Shape:
    def __init__(self, rows, cols, points, size_x, size_y, near):
        self.rows, self.cols, self.points = rows, cols, points
        self.size_x, self.size_y, self.near = size_x, size_y, near
        self.ext_rows = rows + 2 * HALO
        self.sub = points // LANES
        self.cell = 3 * self.sub
        self.left = self.ext_rows * cols
        self.right = self.left + self.ext_rows * HALO
        self.slots = self.right + self.ext_rows * HALO


def cell_slot(shape, gid, me_x, me_y):
    all_rows, all_cols = shape.rows * shape.size_x, shape.cols * shape.size_y
    grid_row = lax.div(gid, jnp.int32(all_cols))
    grid_col = gid - grid_row * all_cols
    row = grid_row - me_x * shape.rows
    row = jnp.where(row < 0, row + all_rows, row)
    row = jnp.where(row >= shape.rows + HALO, row - all_rows + shape.ext_rows, row)
    col = grid_col - me_y * shape.cols + HALO
    col = jnp.where(col < 0, col + all_cols, col)
    col = jnp.where(col >= all_cols, col - all_cols, col)
    middle = row * shape.cols + col - HALO
    left = shape.left + row * HALO + col
    right = shape.right + row * HALO + col - HALO - shape.cols
    slot = jnp.where(col < HALO, left, jnp.where(col >= HALO + shape.cols, right, middle))
    return jnp.clip(slot, 0, shape.slots - 1)


def cell_points(ref, slot, shape):
    block = ref[slot]
    return [block[i * shape.sub : (i + 1) * shape.sub] for i in range(3)]


def put_rows(ref, sub, first, values):
    for i, value in enumerate(values):
        ref[(first + i) * sub : (first + i + 1) * sub, :] = value


def prepare_source(y, f, side_ref, coef_ref, gs_ref, gc_ref, base, shape):
    sub = shape.sub
    square = y[0] * y[0] + y[1] * y[1] + y[2] * y[2]
    split = [pieces(v) for v in (-2.0 * y[0], -2.0 * y[1], -2.0 * y[2], square + soften)]
    for p in range(3):
        rows = [split[0][p], split[1][p], split[2][p]]
        put_rows(gs_ref, sub, 8 * p, rows)
        put_rows(gs_ref, sub, 8 * p + 4, [split[3][p]])
    along = y[0] * f[0] + y[1] * f[1] + y[2] * f[2]
    line = [f[0], f[1], f[2], along]
    values = list(line)
    for i in range(3):
        values += [y[i] * v for v in line]
    values += [square * v for v in f]
    count = len(values)
    for r, value in enumerate(values):
        for p, piece in enumerate(pieces(value)):
            put_rows(gc_ref, sub, p * count + r, [piece])
    for k in range(sub):
        h, m, l = [strided(gs_ref, p * 8 * sub + k, 8, sub) for p in range(3)]
        block = jnp.concatenate([h, m, h, l, h, m], axis=0).T.astype(bf16)
        side_ref[base + k * LANES : base + (k + 1) * LANES, :] = block
        rows = strided(gc_ref, k, coef_ref.shape[0], sub)
        coef_ref[:, base + k * LANES : base + (k + 1) * LANES] = rows.astype(bf16)


def finish(x, total):
    line = x[0] * total(0) + x[1] * total(1) + x[2] * total(2) - total(3)
    square = x[0] * x[0] + x[1] * x[1] + x[2] * x[2] + 2.0 * soften
    low = [total(i) for i in range(3)]
    near = [[total(4 + 4 * j + i) for i in range(4)] for j in range(3)]
    far = [total(16 + i) for i in range(3)]
    out = []
    for i in range(3):
        cross = x[0] * near[0][i] + x[1] * near[1][i] + x[2] * near[2][i]
        turned = x[0] * near[i][0] + x[1] * near[i][1] + x[2] * near[i][2] - near[i][3]
        direct = square * low[i] + far[i] - 2.0 * cross
        out.append(stokes_scale * (direct + x[i] * line - turned))
    return out


COEF = 19


def mega_kernel(
    shape,
    listed,
    near_ref,
    drag_ref,
    pos_ref,
    analysis_hbm,
    stiffness_ref,
    synthesis_hbm,
    wpos_ref,
    wnormal_ref,
    wweight_ref,
    wdensity_ref,
    pnear_ref,
    cpatch_ref,
    moved_ref,
    dens_ref,
    analysis_ref,
    synthesis_ref,
    e_ref,
    f_ref,
    v_ref,
    gs_ref,
    gc_ref,
    gt_ref,
    side_ref,
    coef_ref,
    feat_ref,
    h_ref,
    hp_ref,
    hn_ref,
    hd_ref,
    hw_ref,
    gd_ref,
    gq_ref,
    gm_ref,
    gf_ref,
    gw_ref,
    lside_ref,
    lmom_ref,
    lfeat_ref,
    wfeat_ref,
    lacc_ref,
    wacc_ref,
    mine_ref,
    row_ref,
    from_y,
    from_x,
    local,
    xsend,
    xrecv,
    ysend,
    yrecv,
    wsend,
    wrecv,
    tsend_y,
    trecv_y,
    tsend_x,
    trecv_x,
):
    me_x, me_y = lax.axis_index("cx"), lax.axis_index("cy")
    e_cells, f_cells = e_ref, f_ref
    e_ref = e_cells.reshape(e_cells.shape[0] * e_cells.shape[1], LANES)
    f_ref = f_cells.reshape(f_cells.shape[0] * f_cells.shape[1], LANES)
    size_x, size_y = shape.size_x, shape.size_y
    rows, cols, sub, cell = shape.rows, shape.cols, shape.sub, shape.cell
    patches, wpoints = wpos_ref.shape[1], wpos_ref.shape[2]
    wtiles = wpoints // LANES

    weights = [
        pltpu.make_async_copy(analysis_hbm, analysis_ref, local.at[0]),
        pltpu.make_async_copy(synthesis_hbm, synthesis_ref, local.at[1]),
    ]
    for copy in weights:
        copy.start()

    def around(step_x, step_y):
        return (lax.rem(me_x + step_x + size_x, size_x), lax.rem(me_y + step_y + size_y, size_y))

    def along_walls(step):
        other = lax.rem(me_x * size_y + me_y + step + size_x * size_y, size_x * size_y)
        there = lax.div(other, jnp.int32(size_y))
        return (there, other - there * size_y)

    peers_y = [around(0, d) for d in range(1, size_y)]
    peers_x = [around(d, 0) for d in range(1, size_x)]
    after, before = along_walls(1), along_walls(-1)
    greeted = peers_y + peers_x + [after, before]
    barrier = pltpu.get_barrier_semaphore()
    for device in greeted:
        pl.semaphore_signal(barrier, inc=1, device_id=device, device_id_type=MESH)

    for r in range(rows):
        for c in range(cols):
            for i in range(3):
                at = ((r * cols + c) * 3 + i) * sub
                e_ref[at : at + sub, :] = strided(pos_ref, (r * 3 + i) * sub * cols + c, sub, cols)
    e_ref[shape.slots * cell :, :] = jnp.zeros_like(e_ref[shape.slots * cell :, :])
    for ref in (gs_ref, gc_ref, gt_ref, gd_ref, gq_ref, gm_ref, gf_ref, gw_ref):
        ref[...] = jnp.zeros_like(ref)
    one = jnp.ones((sub, LANES), f32)
    gs_ref[3 * sub : 4 * sub, :] = one
    gt_ref[4 * sub : 5 * sub, :] = one

    pl.semaphore_wait(barrier, len(greeted))

    def remote(src, dst, send, recv, device):
        return pltpu.make_async_remote_copy(
            src_ref=src,
            dst_ref=dst,
            send_sem=send,
            recv_sem=recv,
            device_id=device,
            device_id_type=MESH,
        )

    def cells(slot, count):
        return e_cells.at[slot : slot + count]

    xs = []
    for j in range(HALO):
        k = 2 * j
        up = remote(
            cells((rows - HALO + j) * cols, cols),
            cells((rows + HALO + j) * cols, cols),
            xsend.at[k], xrecv.at[k], around(1, 0),
        )
        down = remote(
            cells(j * cols, cols), cells((rows + j) * cols, cols),
            xsend.at[k + 1], xrecv.at[k + 1], around(-1, 0),
        )
        xs += [(up, rows + HALO + j), (down, rows + j)]

    def sideways(row):
        right = remote(
            cells(row * cols + cols - HALO, HALO), cells(shape.left + row * HALO, HALO),
            ysend.at[2 * row], yrecv.at[2 * row], around(0, 1),
        )
        left = remote(
            cells(row * cols, HALO), cells(shape.right + row * HALO, HALO),
            ysend.at[2 * row + 1], yrecv.at[2 * row + 1], around(0, -1),
        )
        return [right, left]

    ws = []
    sources = ((wpos_ref, hp_ref), (wnormal_ref, hn_ref), (wdensity_ref, hd_ref), (wweight_ref, hw_ref))
    for b, device in enumerate((after, before)):
        for src, dst in sources:
            k = len(ws)
            ws.append(remote(src, dst.at[b], wsend.at[k], wrecv.at[k], device))

    for copy, _ in xs:
        copy.start()
    for copy in ws:
        copy.start()
    ys = []
    for row in range(rows):
        for copy in sideways(row):
            copy.start()
            ys.append(copy)

    x = [wpos_ref[i] for i in range(3)]
    lone = jnp.ones((patches, wpoints), f32)
    squares = [x[i] * x[i] for i in range(3)]
    mono = x + [lone] + squares + [x[0] * x[1], x[0] * x[2], x[1] * x[2]]
    square = squares[0] + squares[1] + squares[2]
    for r, value in enumerate(mono):
        for p, piece in enumerate(pieces(value)):
            put_wide(gf_ref, (16 * p + r) * patches, piece)
    for r, value in enumerate(x + [square, lone]):
        for p, piece in enumerate(pieces(value)):
            put_wide(gw_ref, (8 * p + r) * patches, piece)
    for q in range(patches):
        h, m, l = [get_wide(gf_ref, wtiles, p * 16 * patches + q, 16, patches) for p in range(3)]
        lfeat_ref[q * 96 : (q + 1) * 96, :] = jnp.concatenate([h, h, m, h, l, m], axis=0).astype(bf16)
        h, m, l = [get_wide(gw_ref, wtiles, p * 8 * patches + q, 8, patches) for p in range(3)]
        wfeat_ref[q * 48 : (q + 1) * 48, :] = jnp.concatenate([h, h, m, h, l, m], axis=0).astype(bf16)

    def wall_sources(b, y, n, v, w):
        w = -layer_scale * w
        v = [w * value for value in v]
        zero = jnp.zeros_like(w)
        ones = jnp.ones_like(w)
        square = y[0] * y[0] + y[1] * y[1] + y[2] * y[2] + soften
        dist = [-2.0 * y[0], -2.0 * y[1], -2.0 * y[2], square, ones, ones, ones]
        a = y[0] * v[0] + y[1] * v[1] + y[2] * v[2]
        c = y[0] * n[0] + y[1] * n[1] + y[2] * n[2]
        quad = [-(v[i] * c + n[i] * a) for i in range(3)] + [a * c]
        quad += [v[i] * n[i] for i in range(3)]
        quad += [v[i] * n[j] + v[j] * n[i] for i, j in ((0, 1), (0, 2), (1, 2))]
        for values, ref in ((dist, gd_ref), (quad, gq_ref)):
            for r, value in enumerate(values):
                for p, piece in enumerate(pieces(value)):
                    put_wide(ref, (16 * p + r) * patches, piece)
        for r, value in enumerate(y + [ones]):
            for p, piece in enumerate(pieces(value)):
                if p == 0 or r < 3:
                    put_wide(gm_ref, (4 * p + r) * patches, piece)

        def one_patch(q, _):
            slot = b * patches + q
            for s, ref in enumerate((gd_ref, gq_ref)):
                for k in range(wtiles):
                    h, m, l = [
                        get_tile(ref, wtiles, k, p * 16 * patches + q, 16, patches) for p in range(3)
                    ]
                    block = jnp.concatenate([h, m, h, l, h, m], axis=0).T.astype(bf16)
                    at = s * wpoints + k * LANES
                    lside_ref[slot, at : at + LANES, :] = block
            rows16 = get_wide(gm_ref, wtiles, q, 16, patches)
            lmom_ref[slot] = rows16.astype(bf16)
            return 0

        lax.fori_loop(0, patches, one_patch, 0)

    wall_sources(
        1, x, [wnormal_ref[i] for i in range(3)], [wdensity_ref[i] for i in range(3)], wweight_ref[...]
    )

    for copy in weights:
        copy.wait()

    def membrane(first, count):
        tiles = [strided(e_ref, first * sub + k, count, sub) for k in range(sub)]
        value = jnp.concatenate(tiles, axis=1)
        centred = (value - jnp.mean(value, axis=1, keepdims=True)).astype(bf16)
        coeff = jnp.dot(centred, analysis_ref[...], preferred_element_type=f32)
        scaled = (coeff * stiffness_ref[...]).astype(bf16)
        force = -jnp.dot(scaled, synthesis_ref[...], preferred_element_type=f32)
        for k in range(sub):
            f_ref[pl.ds(first * sub + k, count, stride=sub), :] = force[:, k * LANES : (k + 1) * LANES]

    membrane(0, 3 * rows * cols)

    for copy in ws:
        copy.wait_recv()
    for b in range(2):
        wall_sources(
            2 * b,
            [hp_ref[b, i] for i in range(3)],
            [hn_ref[b, i] for i in range(3)],
            [hd_ref[b, i] for i in range(3)],
            hw_ref[b],
        )

    for copy, row in xs:
        copy.wait_recv()
        for onward in sideways(row):
            onward.start()
            ys.append(onward)

    all_patches = patches * size_x * size_y
    block_start = (me_x * size_y + me_y) * patches

    def put_patch(ref, t, value):
        height = ref.shape[0] // wtiles
        for k in range(wtiles):
            at = pl.multiple_of(k * height + t * value.shape[0], 8)
            ref[pl.ds(at, value.shape[0]), :] = value[:, k * LANES : (k + 1) * LANES]

    def layer_patch(t, _):
        feat = lfeat_ref[pl.ds(pl.multiple_of(t * 96, 16), 96), :]
        total = None
        for n in range(listed + 1):
            if n == 0:
                slot = t + patches
            else:
                slot = pnear_ref[n - 1, t] - block_start + patches
                slot = jnp.where(slot < 0, slot + all_patches, slot)
                slot = jnp.where(slot >= all_patches, slot - all_patches, slot)
                slot = jnp.clip(slot, 0, 3 * patches - 1)
            side = lside_ref[slot]
            both = jnp.dot(side, feat, preferred_element_type=f32)
            root = lax.rsqrt(both[:wpoints])
            square = root * root
            scalar = (both[wpoints:] * (square * square * root)).astype(bf16)
            moment = lmom_ref[slot]
            part = jnp.dot(moment, scalar, preferred_element_type=f32)
            total = part if total is None else total + part
        put_patch(lacc_ref, t, total)
        return 0

    lax.fori_loop(0, patches, layer_patch, 0)

    membrane(3 * rows * cols, 3 * 2 * HALO * cols)
    for copy in ys:
        copy.wait_recv()
    membrane(3 * shape.left, -(-3 * (shape.slots - shape.left) // 8) * 8)

    def cell_step(i, best):
        r = lax.div(i, jnp.int32(cols))
        c = i - r * cols
        x = cell_points(e_cells, i, shape)
        square = x[0] * x[0] + x[1] * x[1] + x[2] * x[2]
        split = [pieces(v) for v in (x[0], x[1], x[2], square)]
        for p in range(3):
            put_rows(gt_ref, sub, 8 * p, [s[p] for s in split])
        for k in range(sub):
            h, m, l = [strided(gt_ref, p * 8 * sub + k, 8, sub) for p in range(3)]
            feat_ref[:, k * LANES : (k + 1) * LANES] = jnp.concatenate(
                [h, h, m, h, l, m], axis=0
            ).astype(bf16)
        for n in range(shape.near):
            slot = cell_slot(shape, near_ref[r, n, c], me_x, me_y)
            prepare_source(
                cell_points(e_cells, slot, shape), cell_points(f_cells, slot, shape),
                side_ref, coef_ref, gs_ref, gc_ref, n * shape.points, shape,
            )
        side = side_ref[...]
        coef = coef_ref[...]
        for t in range(shape.points // WIDTH):
            root = lax.rsqrt(
                jnp.dot(side, feat_ref[:, t * WIDTH : (t + 1) * WIDTH], preferred_element_type=f32)
            )
            cube = (root * root * root).astype(bf16)
            acc = jnp.dot(coef, cube, preferred_element_type=f32)
            for k in range(WIDTH // LANES):
                tile = t * (WIDTH // LANES) + k
                h_ref[pl.ds(tile, acc.shape[0], stride=sub), :] = acc[:, k * LANES : (k + 1) * LANES]

        def total(row):
            a, b, d = [h_ref[(p * COEF + row) * sub : (p * COEF + row + 1) * sub, :] for p in range(3)]
            return a + (b + d)

        parts = finish(x, total)
        own = cell_points(f_cells, i, shape)
        drag = drag_ref[r, c]
        squared = jnp.zeros_like(best)
        values = []
        for k in range(3):
            value = drag * own[k] + parts[k]
            values.append(value)
            squared = squared + value * value
        v_ref[pl.ds(pl.multiple_of(i * cell, 8), cell), :] = jnp.concatenate(values, axis=0)
        return jnp.maximum(best, squared)

    best = lax.fori_loop(0, rows * cols, cell_step, jnp.zeros((sub, LANES), f32))
    mine_ref[...] = best

    def wall_step(t, _):
        for n in range(cpatch_ref.shape[0]):
            slot = cell_slot(shape, cpatch_ref[n, t], me_x, me_y)
            prepare_source(
                cell_points(e_cells, slot, shape), cell_points(f_cells, slot, shape),
                side_ref, coef_ref, gs_ref, gc_ref, n * shape.points, shape,
            )
        feat = wfeat_ref[pl.ds(pl.multiple_of(t * 48, 16), 48), :]
        acc = None
        for n in range(cpatch_ref.shape[0]):
            part = slice(n * shape.points, (n + 1) * shape.points)
            root = lax.rsqrt(jnp.dot(side_ref[part, :], feat, preferred_element_type=f32))
            cube = (root * root * root).astype(bf16)
            more = jnp.dot(coef_ref[:, part], cube, preferred_element_type=f32)
            acc = more if acc is None else acc + more
        put_patch(wacc_ref, t, acc)
        return 0

    lax.fori_loop(0, 1, wall_step, 0)
    copies = []
    for d, device in enumerate(peers_y):
        copies.append(remote(mine_ref, from_y.at[d], tsend_y.at[d], trecv_y.at[d], device))
        copies[-1].start()
    lax.fori_loop(1, patches // 2, wall_step, 0)
    best = mine_ref[...]
    for d, copy in enumerate(copies):
        copy.wait_recv()
        best = jnp.maximum(best, from_y[d])
    row_ref[...] = best
    lax.fori_loop(patches // 2, patches // 2 + 1, wall_step, 0)
    for d, device in enumerate(peers_x):
        copies.append(remote(row_ref, from_x.at[d], tsend_x.at[d], trecv_x.at[d], device))
        copies[-1].start()
    lax.fori_loop(patches // 2 + 1, patches, wall_step, 0)

    def wall_total(row):
        a, b, d = [
            get_wide(wacc_ref, wtiles, p * COEF + row, patches, coef_ref.shape[0]) for p in range(3)
        ]
        return a + (b + d)

    flow = finish(x, wall_total)
    moment = [get_wide(lacc_ref, wtiles, r, patches, 16) for r in range(11)]
    moment = [moment[i] + (moment[4 + i] + moment[8 + i]) for i in range(3)] + [moment[3]]
    for i in range(3):
        layer = x[i] * moment[3] - moment[i]
        dens_ref[i] = 2.0 * layer + 2.0 * flow[i]

    best = row_ref[...]
    for d, copy in enumerate(copies[size_y - 1 :]):
        copy.wait_recv()
        best = jnp.maximum(best, from_x[d])
    top = jnp.sqrt(jnp.max(best, keepdims=True))
    step = 1.0 / (top + 1e-06)
    for r in range(rows):
        for c in range(cols):
            for i in range(3):
                at = ((r * cols + c) * 3 + i) * sub
                value = e_ref[at : at + sub, :] + step * v_ref[at : at + sub, :]
                moved_ref[pl.ds((r * 3 + i) * sub * cols + c, sub, stride=cols), :] = value
    for copy, _ in xs:
        copy.wait_send()
    for copy in ws + ys + copies:
        copy.wait_send()


def body(
    cell_pos,
    cell_drag,
    cell_near,
    analysis,
    stiffness,
    synthesis,
    wall_pos,
    wall_normal,
    wall_weight,
    density,
    patch_near,
    cell_to_patch,
):
    rows, cols, _, points = cell_pos.shape
    size_x, size_y = lax.axis_size("cx"), lax.axis_size("cy")
    near = cell_near.shape[2]
    listed = patch_near.shape[1]
    patches, _, wpoints = wall_pos.shape
    shape = Shape(rows, cols, points, size_x, size_y, near)
    sub, cell = shape.sub, shape.cell
    raw = cell_pos.reshape(rows, cols, 3, sub, LANES)
    raw = jnp.transpose(raw, (0, 2, 3, 1, 4)).reshape(rows * 3 * sub * cols, LANES)
    wtiles = wpoints // LANES
    spare = -(-shape.slots // 8) * 8
    sources = near * points
    assert cell_to_patch.shape[1] == near
    coef_rows = -(-3 * COEF // 16) * 16
    dma = pltpu.SemaphoreType.DMA
    vmem = pltpu.VMEM
    in_vmem = pl.BlockSpec(memory_space=pltpu.VMEM)
    in_smem = pl.BlockSpec(memory_space=pltpu.SMEM)
    in_hbm = pl.BlockSpec(memory_space=pl.ANY)
    walls = lambda v: jnp.transpose(v, (1, 0, 2))
    moved, dens = pl.pallas_call(
        functools.partial(mega_kernel, shape, listed),
        out_shape=(
            jax.ShapeDtypeStruct(raw.shape, f32),
            jax.ShapeDtypeStruct((3, patches, wpoints), f32),
        ),
        in_specs=[
            in_smem, in_smem, in_vmem, in_hbm, in_vmem, in_hbm,
            in_vmem, in_vmem, in_vmem, in_vmem, in_smem, in_smem,
        ],
        out_specs=[in_vmem, in_vmem],
        scratch_shapes=[
            vmem(analysis.shape, bf16),
            vmem(synthesis.shape, bf16),
            vmem((spare, cell, LANES), f32),
            vmem((spare, cell, LANES), f32),
            vmem((rows * cols * cell, LANES), f32),
            vmem((24 * sub, LANES), f32),
            vmem((coef_rows * sub, LANES), f32),
            vmem((24 * sub, LANES), f32),
            vmem((sources, 48), bf16),
            vmem((coef_rows, sources), bf16),
            vmem((48, points), bf16),
            vmem((coef_rows * sub, LANES), f32),
            vmem((2, 3, patches, wpoints), f32),
            vmem((2, 3, patches, wpoints), f32),
            vmem((2, 3, patches, wpoints), f32),
            vmem((2, patches, wpoints), f32),
            vmem((48 * patches * wtiles, LANES), f32),
            vmem((48 * patches * wtiles, LANES), f32),
            vmem((16 * patches * wtiles, LANES), f32),
            vmem((48 * patches * wtiles, LANES), f32),
            vmem((24 * patches * wtiles, LANES), f32),
            vmem((3 * patches, 2 * wpoints, 96), bf16),
            vmem((3 * patches, 16, wpoints), bf16),
            vmem((patches * 96, wpoints), bf16),
            vmem((patches * 48, wpoints), bf16),
            vmem((patches * 16 * wtiles, LANES), f32),
            vmem((patches * coef_rows * wtiles, LANES), f32),
            vmem((sub, LANES), f32),
            vmem((sub, LANES), f32),
            vmem((size_y - 1, sub, LANES), f32),
            vmem((size_x - 1, sub, LANES), f32),
            dma((2,)),
            dma((2 * HALO,)),
            dma((2 * HALO,)),
            dma((2 * shape.ext_rows,)),
            dma((2 * shape.ext_rows,)),
            dma((8,)),
            dma((8,)),
            dma((size_y - 1,)),
            dma((size_y - 1,)),
            dma((size_x - 1,)),
            dma((size_x - 1,)),
        ],
        compiler_params=pltpu.CompilerParams(
            collective_id=0, has_side_effects=True, vmem_limit_bytes=56 * 2**20
        ),
        name="mega",
    )(
        jnp.transpose(cell_near, (0, 2, 1)),
        cell_drag,
        raw,
        analysis,
        stiffness[None, :],
        synthesis,
        walls(wall_pos),
        walls(wall_normal),
        wall_weight,
        walls(density),
        jnp.transpose(patch_near),
        jnp.transpose(cell_to_patch),
    )
    moved = jnp.transpose(moved.reshape(rows, 3, sub, cols, LANES), (0, 3, 1, 2, 4))
    return moved.reshape(cell_pos.shape), jnp.transpose(dens, (1, 0, 2))


def solution(mesh):
    placed = (
        P("cx", "cy", None, None),
        P("cx", "cy"),
        P("cx", "cy", None),
        P(),
        P(),
        P(),
        P(("cx", "cy"), None, None),
        P(("cx", "cy"), None, None),
        P(("cx", "cy"), None),
        P(("cx", "cy"), None, None),
        P(("cx", "cy"), None),
        P(("cx", "cy"), None),
    )
    return jax.shard_map(
        body,
        mesh=mesh,
        in_specs=placed,
        out_specs=(P("cx", "cy", None, None), P(("cx", "cy"), None, None)),
        check_vma=False,
    )
```

```python
import functools
import math

import jax
import jax.numpy as jnp
from jax import lax
from jax.experimental import pallas as pl
from jax.experimental.pallas import tpu as pltpu
from jax.sharding import PartitionSpec as P

HALO = 3
LANES = 128
WIDTH = 512

soften = 0.25
stokes_scale = 1.0 / (8.0 * math.pi)
layer_scale = 3.0 / (4.0 * math.pi)

MESH = pl.DeviceIdType.MESH
f32 = jnp.float32
bf16 = jnp.bfloat16


def pieces(value):
    high = value.astype(bf16).astype(f32)
    rest = value - high
    middle = rest.astype(bf16).astype(f32)
    return high, middle, rest - middle


def strided(ref, start, count, stride):
    return ref[pl.ds(start, count, stride=stride), :]


def put_wide(ref, first, value):
    tiles = value.shape[1] // LANES
    height = ref.shape[0] // tiles
    for k in range(tiles):
        at = k * height + first
        ref[at : at + value.shape[0], :] = value[:, k * LANES : (k + 1) * LANES]


def get_tile(ref, tiles, tile, start, count, stride):
    height = ref.shape[0] // tiles
    return ref[pl.ds(tile * height + start, count, stride=stride), :]


def get_wide(ref, tiles, start, count, stride):
    return jnp.concatenate([get_tile(ref, tiles, k, start, count, stride) for k in range(tiles)], axis=1)


class Shape:
    def __init__(self, rows, cols, points, size_x, size_y, near):
        self.rows, self.cols, self.points = rows, cols, points
        self.size_x, self.size_y, self.near = size_x, size_y, near
        self.ext_rows = rows + 2 * HALO
        self.sub = points // LANES
        self.cell = 3 * self.sub
        self.left = self.ext_rows * cols
        self.right = self.left + self.ext_rows * HALO
        self.slots = self.right + self.ext_rows * HALO


def cell_slot(shape, gid, me_x, me_y):
    all_rows, all_cols = shape.rows * shape.size_x, shape.cols * shape.size_y
    grid_row = lax.div(gid, jnp.int32(all_cols))
    grid_col = gid - grid_row * all_cols
    row = grid_row - me_x * shape.rows
    row = jnp.where(row < 0, row + all_rows, row)
    row = jnp.where(row >= shape.rows + HALO, row - all_rows + shape.ext_rows, row)
    col = grid_col - me_y * shape.cols + HALO
    col = jnp.where(col < 0, col + all_cols, col)
    col = jnp.where(col >= all_cols, col - all_cols, col)
    middle = row * shape.cols + col - HALO
    left = shape.left + row * HALO + col
    right = shape.right + row * HALO + col - HALO - shape.cols
    slot = jnp.where(col < HALO, left, jnp.where(col >= HALO + shape.cols, right, middle))
    return jnp.clip(slot, 0, shape.slots - 1)


def cell_points(ref, slot, shape):
    block = ref[slot]
    return [block[i * shape.sub : (i + 1) * shape.sub] for i in range(3)]


def put_rows(ref, sub, first, values):
    for i, value in enumerate(values):
        ref[(first + i) * sub : (first + i + 1) * sub, :] = value


def prepare_source(y, f, side_ref, coef_ref, gs_ref, gc_ref, base, shape):
    sub = shape.sub
    square = y[0] * y[0] + y[1] * y[1] + y[2] * y[2]
    split = [pieces(v) for v in (-2.0 * y[0], -2.0 * y[1], -2.0 * y[2], square + soften)]
    for p in range(3):
        rows = [split[0][p], split[1][p], split[2][p]]
        put_rows(gs_ref, sub, 8 * p, rows)
        put_rows(gs_ref, sub, 8 * p + 4, [split[3][p]])
    along = y[0] * f[0] + y[1] * f[1] + y[2] * f[2]
    line = [f[0], f[1], f[2], along]
    values = list(line)
    for i in range(3):
        values += [y[i] * v for v in line]
    values += [square * v for v in f]
    count = len(values)
    for r, value in enumerate(values):
        for p, piece in enumerate(pieces(value)):
            put_rows(gc_ref, sub, p * count + r, [piece])
    for k in range(sub):
        h, m, l = [strided(gs_ref, p * 8 * sub + k, 8, sub) for p in range(3)]
        block = jnp.concatenate([h, m, h, l, h, m], axis=0).T.astype(bf16)
        side_ref[base + k * LANES : base + (k + 1) * LANES, :] = block
        rows = strided(gc_ref, k, coef_ref.shape[0], sub)
        coef_ref[:, base + k * LANES : base + (k + 1) * LANES] = rows.astype(bf16)


def finish(x, total):
    line = x[0] * total(0) + x[1] * total(1) + x[2] * total(2) - total(3)
    square = x[0] * x[0] + x[1] * x[1] + x[2] * x[2] + 2.0 * soften
    low = [total(i) for i in range(3)]
    near = [[total(4 + 4 * j + i) for i in range(4)] for j in range(3)]
    far = [total(16 + i) for i in range(3)]
    out = []
    for i in range(3):
        cross = x[0] * near[0][i] + x[1] * near[1][i] + x[2] * near[2][i]
        turned = x[0] * near[i][0] + x[1] * near[i][1] + x[2] * near[i][2] - near[i][3]
        direct = square * low[i] + far[i] - 2.0 * cross
        out.append(stokes_scale * (direct + x[i] * line - turned))
    return out


COEF = 19


def mega_kernel(
    shape,
    listed,
    near_ref,
    drag_ref,
    pos_ref,
    analysis_hbm,
    stiffness_ref,
    synthesis_hbm,
    wpos_ref,
    wnormal_ref,
    wweight_ref,
    wdensity_ref,
    pnear_ref,
    cpatch_ref,
    speed_ref,
    top_ref,
    half_ref,
    analysis_ref,
    synthesis_ref,
    e_ref,
    f_ref,
    v_ref,
    gs_a,
    gs_b,
    gc_a,
    gc_b,
    gt_ref,
    side_ref,
    coef_ref,
    feats_ref,
    cube_a,
    cube_b,
    h_ref,
    hp_ref,
    hn_ref,
    hd_ref,
    hw_ref,
    gd_ref,
    gq_ref,
    gm_ref,
    gf_ref,
    gw_ref,
    lside_ref,
    lmom_ref,
    lfeat_ref,
    wfeat_ref,
    lacc_ref,
    wacc_ref,
    mine_ref,
    row_ref,
    from_y,
    from_x,
    local,
    xsend,
    xrecv,
    ysend,
    yrecv,
    wsend,
    wrecv,
    tsend_y,
    trecv_y,
    tsend_x,
    trecv_x,
):
    me_x, me_y = lax.axis_index("cx"), lax.axis_index("cy")
    e_cells, f_cells = e_ref, f_ref
    e_ref = e_cells.reshape(e_cells.shape[0] * e_cells.shape[1], LANES)
    f_ref = f_cells.reshape(f_cells.shape[0] * f_cells.shape[1], LANES)
    gs, gc, cubes = (gs_a, gs_b), (gc_a, gc_b), (cube_a, cube_b)
    size_x, size_y = shape.size_x, shape.size_y
    rows, cols, sub, cell = shape.rows, shape.cols, shape.sub, shape.cell
    patches, wpoints = wpos_ref.shape[1], wpos_ref.shape[2]
    wtiles = wpoints // LANES

    weights = [
        pltpu.make_async_copy(analysis_hbm, analysis_ref, local.at[0]),
        pltpu.make_async_copy(synthesis_hbm, synthesis_ref, local.at[1]),
    ]
    for copy in weights:
        copy.start()

    def around(step_x, step_y):
        return (lax.rem(me_x + step_x + size_x, size_x), lax.rem(me_y + step_y + size_y, size_y))

    def along_walls(step):
        other = lax.rem(me_x * size_y + me_y + step + size_x * size_y, size_x * size_y)
        there = lax.div(other, jnp.int32(size_y))
        return (there, other - there * size_y)

    peers_y = [around(0, d) for d in range(1, size_y)]
    peers_x = [around(d, 0) for d in range(1, size_x)]
    after, before = along_walls(1), along_walls(-1)
    greeted = peers_y + peers_x + [after, before]
    barrier = pltpu.get_barrier_semaphore()
    for device in greeted:
        pl.semaphore_signal(barrier, inc=1, device_id=device, device_id_type=MESH)

    for r in range(rows):
        for c in range(cols):
            for i in range(3):
                at = ((r * cols + c) * 3 + i) * sub
                e_ref[at : at + sub, :] = strided(pos_ref, (r * 3 + i) * sub * cols + c, sub, cols)
    e_ref[shape.slots * cell :, :] = jnp.zeros_like(e_ref[shape.slots * cell :, :])
    for ref in (*gs, *gc, gt_ref, gd_ref, gq_ref, gm_ref, gf_ref, gw_ref):
        ref[...] = jnp.zeros_like(ref)
    one = jnp.ones((sub, LANES), f32)
    for ref in gs:
        ref[3 * sub : 4 * sub, :] = one
    gt_ref[4 * sub : 5 * sub, :] = one

    pl.semaphore_wait(barrier, len(greeted))

    def remote(src, dst, send, recv, device):
        return pltpu.make_async_remote_copy(
            src_ref=src,
            dst_ref=dst,
            send_sem=send,
            recv_sem=recv,
            device_id=device,
            device_id_type=MESH,
        )

    def cells(slot, count):
        return e_cells.at[slot : slot + count]

    xs = []
    for j in range(HALO):
        k = 2 * j
        up = remote(
            cells((rows - HALO + j) * cols, cols),
            cells((rows + HALO + j) * cols, cols),
            xsend.at[k], xrecv.at[k], around(1, 0),
        )
        down = remote(
            cells(j * cols, cols), cells((rows + j) * cols, cols),
            xsend.at[k + 1], xrecv.at[k + 1], around(-1, 0),
        )
        xs += [(up, rows + HALO + j), (down, rows + j)]

    def sideways(row):
        right = remote(
            cells(row * cols + cols - HALO, HALO), cells(shape.left + row * HALO, HALO),
            ysend.at[2 * row], yrecv.at[2 * row], around(0, 1),
        )
        left = remote(
            cells(row * cols, HALO), cells(shape.right + row * HALO, HALO),
            ysend.at[2 * row + 1], yrecv.at[2 * row + 1], around(0, -1),
        )
        return [right, left]

    ws = []
    sources = ((wpos_ref, hp_ref), (wnormal_ref, hn_ref), (wdensity_ref, hd_ref), (wweight_ref, hw_ref))
    for b, device in enumerate((after, before)):
        for src, dst in sources:
            k = len(ws)
            ws.append(remote(src, dst.at[b], wsend.at[k], wrecv.at[k], device))

    for copy, _ in xs:
        copy.start()
    for copy in ws:
        copy.start()
    ys = []
    for row in range(rows):
        for copy in sideways(row):
            copy.start()
            ys.append(copy)

    def target(i, _):
        x = cell_points(e_cells, i, shape)
        square = x[0] * x[0] + x[1] * x[1] + x[2] * x[2]
        split = [pieces(v) for v in (x[0], x[1], x[2], square)]
        for p in range(3):
            put_rows(gt_ref, sub, 8 * p, [s[p] for s in split])
        tiles = []
        for k in range(sub):
            h, m, l = [strided(gt_ref, p * 8 * sub + k, 8, sub) for p in range(3)]
            tiles.append(jnp.concatenate([h, h, m, h, l, m], axis=0).astype(bf16))
        feats_ref[i] = jnp.concatenate(tiles, axis=1)
        return 0

    lax.fori_loop(0, rows * cols, target, 0)

    x = [wpos_ref[i] for i in range(3)]
    lone = jnp.ones((patches, wpoints), f32)
    squares = [x[i] * x[i] for i in range(3)]
    mono = x + [lone] + squares + [x[0] * x[1], x[0] * x[2], x[1] * x[2]]
    square = squares[0] + squares[1] + squares[2]
    for r, value in enumerate(mono):
        for p, piece in enumerate(pieces(value)):
            put_wide(gf_ref, (16 * p + r) * patches, piece)
    for r, value in enumerate(x + [square, lone]):
        for p, piece in enumerate(pieces(value)):
            put_wide(gw_ref, (8 * p + r) * patches, piece)
    for q in range(patches):
        h, m, l = [get_wide(gf_ref, wtiles, p * 16 * patches + q, 16, patches) for p in range(3)]
        lfeat_ref[q * 96 : (q + 1) * 96, :] = jnp.concatenate([h, h, m, h, l, m], axis=0).astype(bf16)
        h, m, l = [get_wide(gw_ref, wtiles, p * 8 * patches + q, 8, patches) for p in range(3)]
        wfeat_ref[q * 48 : (q + 1) * 48, :] = jnp.concatenate([h, h, m, h, l, m], axis=0).astype(bf16)

    def wall_sources(b, y, n, v, w):
        w = -layer_scale * w
        v = [w * value for value in v]
        zero = jnp.zeros_like(w)
        ones = jnp.ones_like(w)
        square = y[0] * y[0] + y[1] * y[1] + y[2] * y[2] + soften
        dist = [-2.0 * y[0], -2.0 * y[1], -2.0 * y[2], square, ones, ones, ones]
        a = y[0] * v[0] + y[1] * v[1] + y[2] * v[2]
        c = y[0] * n[0] + y[1] * n[1] + y[2] * n[2]
        quad = [-(v[i] * c + n[i] * a) for i in range(3)] + [a * c]
        quad += [v[i] * n[i] for i in range(3)]
        quad += [v[i] * n[j] + v[j] * n[i] for i, j in ((0, 1), (0, 2), (1, 2))]
        for values, ref in ((dist, gd_ref), (quad, gq_ref)):
            for r, value in enumerate(values):
                for p, piece in enumerate(pieces(value)):
                    put_wide(ref, (16 * p + r) * patches, piece)
        for r, value in enumerate(y + [ones]):
            for p, piece in enumerate(pieces(value)):
                if p == 0 or r < 3:
                    put_wide(gm_ref, (4 * p + r) * patches, piece)

        def one_patch(q, _):
            slot = b * patches + q
            for s, ref in enumerate((gd_ref, gq_ref)):
                for k in range(wtiles):
                    h, m, l = [
                        get_tile(ref, wtiles, k, p * 16 * patches + q, 16, patches) for p in range(3)
                    ]
                    block = jnp.concatenate([h, m, h, l, h, m], axis=0).T.astype(bf16)
                    at = s * wpoints + k * LANES
                    lside_ref[slot, at : at + LANES, :] = block
            rows16 = get_wide(gm_ref, wtiles, q, 16, patches)
            lmom_ref[slot] = rows16.astype(bf16)
            return 0

        lax.fori_loop(0, patches, one_patch, 0)

    wall_sources(
        1, x, [wnormal_ref[i] for i in range(3)], [wdensity_ref[i] for i in range(3)], wweight_ref[...]
    )

    for copy in weights:
        copy.wait()

    def membrane(first, count):
        tiles = [strided(e_ref, first * sub + k, count, sub) for k in range(sub)]
        value = jnp.concatenate(tiles, axis=1)
        centred = (value - jnp.mean(value, axis=1, keepdims=True)).astype(bf16)
        coeff = jnp.dot(centred, analysis_ref[...], preferred_element_type=f32)
        scaled = (coeff * stiffness_ref[...]).astype(bf16)
        force = -jnp.dot(scaled, synthesis_ref[...], preferred_element_type=f32)
        for k in range(sub):
            f_ref[pl.ds(first * sub + k, count, stride=sub), :] = force[:, k * LANES : (k + 1) * LANES]

    membrane(0, 3 * rows * cols)

    for copy in ws:
        copy.wait_recv()
    for b in range(2):
        wall_sources(
            2 * b,
            [hp_ref[b, i] for i in range(3)],
            [hn_ref[b, i] for i in range(3)],
            [hd_ref[b, i] for i in range(3)],
            hw_ref[b],
        )

    def pass_on(pairs):
        for copy, row in pairs:
            copy.wait_recv()
            for onward in sideways(row):
                onward.start()
                ys.append(onward)

    all_patches = patches * size_x * size_y
    block_start = (me_x * size_y + me_y) * patches

    def put_patch(ref, t, value):
        height = ref.shape[0] // wtiles
        for k in range(wtiles):
            at = pl.multiple_of(k * height + t * value.shape[0], 8)
            ref[pl.ds(at, value.shape[0]), :] = value[:, k * LANES : (k + 1) * LANES]

    def layer_patch(t, _):
        feat = lfeat_ref[pl.ds(pl.multiple_of(t * 96, 16), 96), :]
        total = None
        for n in range(listed + 1):
            if n == 0:
                slot = t + patches
            else:
                slot = pnear_ref[n - 1, t] - block_start + patches
                slot = jnp.where(slot < 0, slot + all_patches, slot)
                slot = jnp.where(slot >= all_patches, slot - all_patches, slot)
                slot = jnp.clip(slot, 0, 3 * patches - 1)
            side = lside_ref[slot]
            both = jnp.dot(side, feat, preferred_element_type=f32)
            root = lax.rsqrt(both[:wpoints])
            square = root * root
            scalar = (both[wpoints:] * (square * square * root)).astype(bf16)
            moment = lmom_ref[slot]
            part = jnp.dot(moment, scalar, preferred_element_type=f32)
            total = part if total is None else total + part
        put_patch(lacc_ref, t, total)
        return 0

    done = 0
    for j in range(HALO):
        pass_on(xs[2 * j : 2 * j + 2])
        upto = patches if j == HALO - 1 else (j + 1) * patches // 4
        lax.fori_loop(done, upto, layer_patch, 0)
        done = upto

    membrane(3 * rows * cols, 3 * 2 * HALO * cols)
    for copy in ys:
        copy.wait_recv()
    membrane(3 * shape.left, -(-3 * (shape.slots - shape.left) // 8) * 8)

    def cell_prepare(i):
        r = lax.div(i, jnp.int32(cols))
        c = i - r * cols
        for n in range(shape.near):
            slot = cell_slot(shape, near_ref[r, n, c], me_x, me_y)
            prepare_source(
                cell_points(e_cells, slot, shape), cell_points(f_cells, slot, shape),
                side_ref, coef_ref, gs[n], gc[n], n * shape.points, shape,
            )

    chunks = shape.points // WIDTH
    sources = shape.near * shape.points
    steps = [slice(at, at + WIDTH) for at in range(0, sources, WIDTH)]

    def weigh(part, cube_ref):
        return jnp.dot(coef_ref[:, part], cube_ref[part, :], preferred_element_type=f32)

    def keep(t, acc):
        for k in range(WIDTH // LANES):
            tile = t * (WIDTH // LANES) + k
            h_ref[pl.ds(tile, acc.shape[0], stride=sub), :] = acc[:, k * LANES : (k + 1) * LANES]

    def cell_sums(i):
        last = None
        for t in range(chunks):
            feat = feats_ref[i, :, t * WIDTH : (t + 1) * WIDTH]
            acc = None
            for part in steps:
                root = lax.rsqrt(jnp.dot(side_ref[part, :], feat, preferred_element_type=f32))
                cubes[t % 2][part, :] = (root * root * root).astype(bf16)
                if t > 0:
                    more = weigh(part, cubes[(t - 1) % 2])
                    acc = more if acc is None else acc + more
            if t > 0:
                keep(t - 1, acc)
        acc = None
        for part in steps:
            more = weigh(part, cubes[(chunks - 1) % 2])
            acc = more if acc is None else acc + more
        keep(chunks - 1, acc)

    def cell_finish(i, best):
        r = lax.div(i, jnp.int32(cols))
        c = i - r * cols
        x = cell_points(e_cells, i, shape)

        def total(row):
            a, b, d = [h_ref[(p * COEF + row) * sub : (p * COEF + row + 1) * sub, :] for p in range(3)]
            return a + (b + d)

        parts = finish(x, total)
        own = cell_points(f_cells, i, shape)
        drag = drag_ref[r, c]
        squared = jnp.zeros_like(best)
        values = []
        for k in range(3):
            value = drag * own[k] + parts[k]
            values.append(value)
            squared = squared + value * value
        v_ref[pl.ds(pl.multiple_of(i * cell, 8), cell), :] = jnp.concatenate(values, axis=0)
        return jnp.maximum(best, squared)

    def cell_step(i, best):
        cell_sums(i)
        cell_prepare(jnp.minimum(i + 1, rows * cols - 1))
        return cell_finish(i, best)

    cell_prepare(jnp.int32(0))
    best = lax.fori_loop(0, rows * cols, cell_step, jnp.zeros((sub, LANES), f32))
    mine_ref[...] = best

    def wall_prepare(t):
        for n in range(cpatch_ref.shape[0]):
            slot = cell_slot(shape, cpatch_ref[n, t], me_x, me_y)
            prepare_source(
                cell_points(e_cells, slot, shape), cell_points(f_cells, slot, shape),
                side_ref, coef_ref, gs[n], gc[n], n * shape.points, shape,
            )

    def wall_step(t, _):
        feat = wfeat_ref[pl.ds(pl.multiple_of(t * 48, 16), 48), :]
        acc = None
        for n in range(cpatch_ref.shape[0]):
            part = slice(n * shape.points, (n + 1) * shape.points)
            root = lax.rsqrt(jnp.dot(side_ref[part, :], feat, preferred_element_type=f32))
            cube = (root * root * root).astype(bf16)
            more = jnp.dot(coef_ref[:, part], cube, preferred_element_type=f32)
            acc = more if acc is None else acc + more
        put_patch(wacc_ref, t, acc)
        wall_prepare(jnp.minimum(t + 1, patches - 1))
        return 0

    wall_prepare(jnp.int32(0))
    copies = []
    for d, device in enumerate(peers_y):
        copies.append(remote(mine_ref, from_y.at[d], tsend_y.at[d], trecv_y.at[d], device))
        copies[-1].start()
    half = patches // 2 - 1
    lax.fori_loop(0, half, wall_step, 0)
    best = mine_ref[...]
    for d, copy in enumerate(copies):
        copy.wait_recv()
        best = jnp.maximum(best, from_y[d])
    row_ref[...] = best
    lax.fori_loop(half, half + 1, wall_step, 0)
    for d, device in enumerate(peers_x):
        copies.append(remote(row_ref, from_x.at[d], tsend_x.at[d], trecv_x.at[d], device))
        copies[-1].start()
    lax.fori_loop(half + 1, patches, wall_step, 0)

    def wall_total(row):
        a, b, d = [
            get_wide(wacc_ref, wtiles, p * COEF + row, patches, coef_ref.shape[0]) for p in range(3)
        ]
        return a + (b + d)

    flow = finish(x, wall_total)
    moment = [get_wide(lacc_ref, wtiles, r, patches, 16) for r in range(11)]
    moment = [moment[i] + (moment[4 + i] + moment[8 + i]) for i in range(3)] + [moment[3]]
    for i in range(3):
        layer = x[i] * moment[3] - moment[i]
        half_ref[i] = layer + flow[i]

    best = row_ref[...]
    for d, copy in enumerate(copies[size_y - 1 :]):
        copy.wait_recv()
        best = jnp.maximum(best, from_x[d])
    top_ref[...] = best
    for r in range(rows):
        for c in range(cols):
            for i in range(3):
                at = ((r * cols + c) * 3 + i) * sub
                speed_ref[pl.ds((r * 3 + i) * sub * cols + c, sub, stride=cols), :] = v_ref[at : at + sub, :]
    for copy, _ in xs:
        copy.wait_send()
    for copy in ws + ys + copies:
        copy.wait_send()


def update_kernel(pos_ref, speed_ref, top_ref, half_ref, moved_ref, dens_ref):
    top = jnp.sqrt(jnp.max(top_ref[...], keepdims=True))
    step = 1.0 / (top + 1e-06)
    moved_ref[...] = pos_ref[...] + step * speed_ref[...]
    dens_ref[...] = 2.0 * half_ref[...]


def body(
    cell_pos,
    cell_drag,
    cell_near,
    analysis,
    stiffness,
    synthesis,
    wall_pos,
    wall_normal,
    wall_weight,
    density,
    patch_near,
    cell_to_patch,
):
    rows, cols, _, points = cell_pos.shape
    size_x, size_y = lax.axis_size("cx"), lax.axis_size("cy")
    near = cell_near.shape[2]
    listed = patch_near.shape[1]
    patches, _, wpoints = wall_pos.shape
    shape = Shape(rows, cols, points, size_x, size_y, near)
    sub, cell = shape.sub, shape.cell
    raw = cell_pos.reshape(rows, cols, 3, sub, LANES)
    raw = jnp.transpose(raw, (0, 2, 3, 1, 4)).reshape(rows * 3 * sub * cols, LANES)
    wtiles = wpoints // LANES
    spare = -(-shape.slots // 8) * 8
    sources = near * points
    assert cell_to_patch.shape[1] == near
    coef_rows = -(-3 * COEF // 16) * 16
    dma = pltpu.SemaphoreType.DMA
    vmem = pltpu.VMEM
    in_vmem = pl.BlockSpec(memory_space=pltpu.VMEM)
    in_smem = pl.BlockSpec(memory_space=pltpu.SMEM)
    in_hbm = pl.BlockSpec(memory_space=pl.ANY)
    walls = lambda v: jnp.transpose(v, (1, 0, 2))
    speed, top, half = pl.pallas_call(
        functools.partial(mega_kernel, shape, listed),
        out_shape=(
            jax.ShapeDtypeStruct(raw.shape, f32),
            jax.ShapeDtypeStruct((sub, LANES), f32),
            jax.ShapeDtypeStruct((3, patches, wpoints), f32),
        ),
        in_specs=[
            in_smem, in_smem, in_vmem, in_hbm, in_vmem, in_hbm,
            in_vmem, in_vmem, in_vmem, in_vmem, in_smem, in_smem,
        ],
        out_specs=[in_vmem] * 3,
        scratch_shapes=[
            vmem(analysis.shape, bf16),
            vmem(synthesis.shape, bf16),
            vmem((spare, cell, LANES), f32),
            vmem((spare, cell, LANES), f32),
            vmem((rows * cols * cell, LANES), f32),
            vmem((24 * sub, LANES), f32),
            vmem((24 * sub, LANES), f32),
            vmem((coef_rows * sub, LANES), f32),
            vmem((coef_rows * sub, LANES), f32),
            vmem((24 * sub, LANES), f32),
            vmem((sources, 48), bf16),
            vmem((coef_rows, sources), bf16),
            vmem((rows * cols, 48, points), bf16),
            vmem((sources, WIDTH), bf16),
            vmem((sources, WIDTH), bf16),
            vmem((coef_rows * sub, LANES), f32),
            vmem((2, 3, patches, wpoints), f32),
            vmem((2, 3, patches, wpoints), f32),
            vmem((2, 3, patches, wpoints), f32),
            vmem((2, patches, wpoints), f32),
            vmem((48 * patches * wtiles, LANES), f32),
            vmem((48 * patches * wtiles, LANES), f32),
            vmem((16 * patches * wtiles, LANES), f32),
            vmem((48 * patches * wtiles, LANES), f32),
            vmem((24 * patches * wtiles, LANES), f32),
            vmem((3 * patches, 2 * wpoints, 96), bf16),
            vmem((3 * patches, 16, wpoints), bf16),
            vmem((patches * 96, wpoints), bf16),
            vmem((patches * 48, wpoints), bf16),
            vmem((patches * 16 * wtiles, LANES), f32),
            vmem((patches * coef_rows * wtiles, LANES), f32),
            vmem((sub, LANES), f32),
            vmem((sub, LANES), f32),
            vmem((size_y - 1, sub, LANES), f32),
            vmem((size_x - 1, sub, LANES), f32),
            dma((2,)),
            dma((2 * HALO,)),
            dma((2 * HALO,)),
            dma((2 * shape.ext_rows,)),
            dma((2 * shape.ext_rows,)),
            dma((8,)),
            dma((8,)),
            dma((size_y - 1,)),
            dma((size_y - 1,)),
            dma((size_x - 1,)),
            dma((size_x - 1,)),
        ],
        compiler_params=pltpu.CompilerParams(
            collective_id=0, has_side_effects=True, vmem_limit_bytes=62 * 2**20
        ),
        name="mega",
    )(
        jnp.transpose(cell_near, (0, 2, 1)),
        cell_drag,
        raw,
        analysis,
        stiffness[None, :],
        synthesis,
        walls(wall_pos),
        walls(wall_normal),
        wall_weight,
        walls(density),
        jnp.transpose(patch_near),
        jnp.transpose(cell_to_patch),
    )
    moved, dens = pl.pallas_call(
        update_kernel,
        out_shape=(
            jax.ShapeDtypeStruct(raw.shape, f32),
            jax.ShapeDtypeStruct((3, patches, wpoints), f32),
        ),
        in_specs=[in_vmem] * 4,
        out_specs=[in_vmem] * 2,
        name="update",
    )(raw, speed, top, half)
    moved = jnp.transpose(moved.reshape(rows, 3, sub, cols, LANES), (0, 3, 1, 2, 4))
    return moved.reshape(cell_pos.shape), jnp.transpose(dens, (1, 0, 2))


def solution(mesh):
    placed = (
        P("cx", "cy", None, None),
        P("cx", "cy"),
        P("cx", "cy", None),
        P(),
        P(),
        P(),
        P(("cx", "cy"), None, None),
        P(("cx", "cy"), None, None),
        P(("cx", "cy"), None),
        P(("cx", "cy"), None, None),
        P(("cx", "cy"), None),
        P(("cx", "cy"), None),
    )
    return jax.shard_map(
        body,
        mesh=mesh,
        in_specs=placed,
        out_specs=(P("cx", "cy", None, None), P(("cx", "cy"), None, None)),
        check_vma=False,
    )
```

```python
import functools
import math

import jax
import jax.numpy as jnp
from jax import lax
from jax.experimental import pallas as pl
from jax.experimental.pallas import tpu as pltpu
from jax.sharding import PartitionSpec as P

HALO = 3
LANES = 128
WIDTH = 512

soften = 0.25
stokes_scale = 1.0 / (8.0 * math.pi)
layer_scale = 3.0 / (4.0 * math.pi)

MESH = pl.DeviceIdType.MESH
f32 = jnp.float32
bf16 = jnp.bfloat16


def pieces(value):
    high = value.astype(bf16).astype(f32)
    rest = value - high
    middle = rest.astype(bf16).astype(f32)
    return high, middle, rest - middle


def strided(ref, start, count, stride):
    return ref[pl.ds(start, count, stride=stride), :]


def put_wide(ref, first, value):
    tiles = value.shape[1] // LANES
    height = ref.shape[0] // tiles
    for k in range(tiles):
        at = k * height + first
        ref[at : at + value.shape[0], :] = value[:, k * LANES : (k + 1) * LANES]


def get_tile(ref, tiles, tile, start, count, stride):
    height = ref.shape[0] // tiles
    return ref[pl.ds(tile * height + start, count, stride=stride), :]


def get_wide(ref, tiles, start, count, stride):
    return jnp.concatenate([get_tile(ref, tiles, k, start, count, stride) for k in range(tiles)], axis=1)


class Shape:
    def __init__(self, rows, cols, points, size_x, size_y, near):
        self.rows, self.cols, self.points = rows, cols, points
        self.size_x, self.size_y, self.near = size_x, size_y, near
        self.ext_rows = rows + 2 * HALO
        self.sub = points // LANES
        self.cell = 3 * self.sub
        self.left = self.ext_rows * cols
        self.right = self.left + self.ext_rows * HALO
        self.slots = self.right + self.ext_rows * HALO


def cell_slot(shape, gid, me_x, me_y):
    all_rows, all_cols = shape.rows * shape.size_x, shape.cols * shape.size_y
    grid_row = lax.div(gid, jnp.int32(all_cols))
    grid_col = gid - grid_row * all_cols
    row = grid_row - me_x * shape.rows
    row = jnp.where(row < 0, row + all_rows, row)
    row = jnp.where(row >= shape.rows + HALO, row - all_rows + shape.ext_rows, row)
    col = grid_col - me_y * shape.cols + HALO
    col = jnp.where(col < 0, col + all_cols, col)
    col = jnp.where(col >= all_cols, col - all_cols, col)
    middle = row * shape.cols + col - HALO
    left = shape.left + row * HALO + col
    right = shape.right + row * HALO + col - HALO - shape.cols
    slot = jnp.where(col < HALO, left, jnp.where(col >= HALO + shape.cols, right, middle))
    return jnp.clip(slot, 0, shape.slots - 1)


def cell_points(ref, slot, shape):
    block = ref[slot]
    return [block[i * shape.sub : (i + 1) * shape.sub] for i in range(3)]


def put_rows(ref, sub, first, values):
    for i, value in enumerate(values):
        ref[(first + i) * sub : (first + i + 1) * sub, :] = value


def prepare_sources(sources, side_ref, coef_ref, gs, gc, shape):
    sub, points = shape.sub, shape.points
    for n, (y, f) in enumerate(sources):
        square = y[0] * y[0] + y[1] * y[1] + y[2] * y[2]
        split = [pieces(v) for v in (-2.0 * y[0], -2.0 * y[1], -2.0 * y[2], square + soften)]
        for p in range(3):
            put_rows(gs[n], sub, 8 * p, [split[0][p], split[1][p], split[2][p]])
            put_rows(gs[n], sub, 8 * p + 4, [split[3][p]])
        along = y[0] * f[0] + y[1] * f[1] + y[2] * f[2]
        line = [f[0], f[1], f[2], along]
        values = list(line)
        for i in range(3):
            values += [y[i] * v for v in line]
        values += [square * v for v in f]
        for r, value in enumerate(values):
            for p, piece in enumerate(pieces(value)):
                put_rows(gc[n], sub, p * COEF + r, [piece])
    for k in range(sub):
        groups = []
        for n in range(len(sources)):
            h, m, l = [strided(gs[n], p * 8 * sub + k, 8, sub) for p in range(3)]
            groups += [h, m, h, l, h, m]
            rows = strided(gc[n], k, coef_ref.shape[0], sub)
            at = n * points + k * LANES
            coef_ref[:, at : at + LANES] = rows.astype(bf16)
        block = jnp.concatenate(groups, axis=0).T.astype(bf16)
        side_ref[k * LANES : (k + 1) * LANES, :] = block


COEF = 19


def finish(x, total):
    line = x[0] * total(0) + x[1] * total(1) + x[2] * total(2) - total(3)
    square = x[0] * x[0] + x[1] * x[1] + x[2] * x[2] + 2.0 * soften
    low = [total(i) for i in range(3)]
    near = [[total(4 + 4 * j + i) for i in range(4)] for j in range(3)]
    far = [total(16 + i) for i in range(3)]
    out = []
    for i in range(3):
        cross = x[0] * near[0][i] + x[1] * near[1][i] + x[2] * near[2][i]
        turned = x[0] * near[i][0] + x[1] * near[i][1] + x[2] * near[i][2] - near[i][3]
        direct = square * low[i] + far[i] - 2.0 * cross
        out.append(stokes_scale * (direct + x[i] * line - turned))
    return out


def mega_kernel(
    shape,
    listed,
    near_ref,
    drag_ref,
    pos_hbm,
    analysis_hbm,
    stiffness_hbm,
    synthesis_hbm,
    wpos_hbm,
    wnormal_hbm,
    wweight_hbm,
    wdensity_hbm,
    pnear_ref,
    cpatch_ref,
    speed_ref,
    top_ref,
    half_ref,
    pos_ref,
    stiffness_ref,
    wpos_ref,
    wnormal_ref,
    wweight_ref,
    wdensity_ref,
    analysis_ref,
    synthesis_ref,
    e_ref,
    f_ref,
    v_ref,
    gs_a,
    gs_b,
    gs_c,
    gs_d,
    gc_a,
    gc_b,
    gc_c,
    gc_d,
    gt_ref,
    side_ref,
    coef_ref,
    side_b,
    coef_b,
    feats_ref,
    cube_a,
    cube_b,
    h_ref,
    hp_ref,
    hn_ref,
    hd_ref,
    hw_ref,
    gd_ref,
    gq_ref,
    gm_ref,
    gf_ref,
    gw_ref,
    lside_ref,
    lmom_ref,
    lfeat_ref,
    wfeat_ref,
    lacc_ref,
    wacc_ref,
    mine_ref,
    row_ref,
    from_y,
    from_x,
    local,
    xsend,
    xrecv,
    ysend,
    yrecv,
    wsend,
    wrecv,
    tsend_y,
    trecv_y,
    tsend_x,
    trecv_x,
):
    me_x, me_y = lax.axis_index("cx"), lax.axis_index("cy")
    e_cells, f_cells = e_ref, f_ref
    e_ref = e_cells.reshape(e_cells.shape[0] * e_cells.shape[1], LANES)
    f_ref = f_cells.reshape(f_cells.shape[0] * f_cells.shape[1], LANES)
    gs, gc, cubes = (gs_a, gs_b), (gc_a, gc_b), (cube_a, cube_b)
    size_x, size_y = shape.size_x, shape.size_y
    rows, cols, sub, cell = shape.rows, shape.cols, shape.sub, shape.cell
    patches, wpoints = wpos_hbm.shape[1], wpos_hbm.shape[2]
    wtiles = wpoints // LANES

    weights = [
        pltpu.make_async_copy(analysis_hbm, analysis_ref, local.at[0]),
        pltpu.make_async_copy(synthesis_hbm, synthesis_ref, local.at[1]),
        pltpu.make_async_copy(stiffness_hbm, stiffness_ref, local.at[2]),
    ]
    pairs = (
        (pos_hbm, pos_ref), (wpos_hbm, wpos_ref), (wnormal_hbm, wnormal_ref),
        (wweight_hbm, wweight_ref), (wdensity_hbm, wdensity_ref),
    )
    inputs = [pltpu.make_async_copy(src, dst, local.at[3 + k]) for k, (src, dst) in enumerate(pairs)]
    for copy in inputs + weights:
        copy.start()

    def around(step_x, step_y):
        return (lax.rem(me_x + step_x + size_x, size_x), lax.rem(me_y + step_y + size_y, size_y))

    def along_walls(step):
        other = lax.rem(me_x * size_y + me_y + step + size_x * size_y, size_x * size_y)
        there = lax.div(other, jnp.int32(size_y))
        return (there, other - there * size_y)

    peers_y = [around(0, d) for d in range(1, size_y)]
    peers_x = [around(d, 0) for d in range(1, size_x)]
    after, before = along_walls(1), along_walls(-1)
    greeted = peers_y + peers_x + [after, before]
    barrier = pltpu.get_barrier_semaphore()
    for device in greeted:
        pl.semaphore_signal(barrier, inc=1, device_id=device, device_id_type=MESH)

    e_ref[shape.slots * cell :, :] = jnp.zeros_like(e_ref[shape.slots * cell :, :])
    for ref in (*gs, gs_c, gs_d, *gc, gc_c, gc_d, gt_ref, gd_ref, gq_ref, gm_ref, gf_ref, gw_ref):
        ref[...] = jnp.zeros_like(ref)
    one = jnp.ones((sub, LANES), f32)
    for ref in (*gs, gs_c, gs_d):
        ref[3 * sub : 4 * sub, :] = one
    gt_ref[4 * sub : 5 * sub, :] = one
    for copy in inputs:
        copy.wait()
    for r in range(rows):
        for c in range(cols):
            for i in range(3):
                at = ((r * cols + c) * 3 + i) * sub
                e_ref[at : at + sub, :] = strided(pos_ref, (r * 3 + i) * sub * cols + c, sub, cols)

    pl.semaphore_wait(barrier, len(greeted))

    def remote(src, dst, send, recv, device):
        return pltpu.make_async_remote_copy(
            src_ref=src,
            dst_ref=dst,
            send_sem=send,
            recv_sem=recv,
            device_id=device,
            device_id_type=MESH,
        )

    def cells(slot, count):
        return e_cells.at[slot : slot + count]

    xs = []
    for j in range(HALO):
        k = 2 * j
        up = remote(
            cells((rows - HALO + j) * cols, cols),
            cells((rows + HALO + j) * cols, cols),
            xsend.at[k], xrecv.at[k], around(1, 0),
        )
        down = remote(
            cells(j * cols, cols), cells((rows + j) * cols, cols),
            xsend.at[k + 1], xrecv.at[k + 1], around(-1, 0),
        )
        xs += [(up, rows + HALO + j), (down, rows + j)]

    def sideways(row):
        right = remote(
            cells(row * cols + cols - HALO, HALO), cells(shape.left + row * HALO, HALO),
            ysend.at[2 * row], yrecv.at[2 * row], around(0, 1),
        )
        left = remote(
            cells(row * cols, HALO), cells(shape.right + row * HALO, HALO),
            ysend.at[2 * row + 1], yrecv.at[2 * row + 1], around(0, -1),
        )
        return [right, left]

    ws = []
    sources = ((wpos_ref, hp_ref), (wnormal_ref, hn_ref), (wdensity_ref, hd_ref), (wweight_ref, hw_ref))
    for b, device in enumerate((after, before)):
        for src, dst in sources:
            k = len(ws)
            ws.append(remote(src, dst.at[b], wsend.at[k], wrecv.at[k], device))

    for copy in ws:
        copy.start()
    for copy, _ in xs:
        copy.start()
    ys = []
    for row in range(rows):
        for copy in sideways(row):
            copy.start()
            ys.append(copy)

    def target(i, _):
        x = cell_points(e_cells, i, shape)
        square = x[0] * x[0] + x[1] * x[1] + x[2] * x[2]
        split = [pieces(v) for v in (x[0], x[1], x[2], square)]
        for p in range(3):
            put_rows(gt_ref, sub, 8 * p, [s[p] for s in split])
        tiles = []
        for k in range(sub):
            h, m, l = [strided(gt_ref, p * 8 * sub + k, 8, sub) for p in range(3)]
            tiles.append(jnp.concatenate([h, h, m, h, l, m], axis=0).astype(bf16))
        first = (shape.near - 1) * 48
        blank = jnp.zeros((first, shape.points), bf16)
        feats_ref[i, :first, :] = blank
        feats_ref[i, first : first + 48, :] = jnp.concatenate(tiles, axis=1)
        feats_ref[i, first + 48 :, :] = blank
        return 0

    lax.fori_loop(0, rows * cols, target, 0)

    x = [wpos_ref[i] for i in range(3)]
    lone = jnp.ones((patches, wpoints), f32)
    squares = [x[i] * x[i] for i in range(3)]
    mono = x + [lone] + squares + [x[0] * x[1], x[0] * x[2], x[1] * x[2]]
    square = squares[0] + squares[1] + squares[2]
    for r, value in enumerate(mono):
        for p, piece in enumerate(pieces(value)):
            put_wide(gf_ref, (16 * p + r) * patches, piece)
    for r, value in enumerate(x + [square, lone]):
        for p, piece in enumerate(pieces(value)):
            put_wide(gw_ref, (8 * p + r) * patches, piece)
    for q in range(patches):
        h, m, l = [get_wide(gf_ref, wtiles, p * 16 * patches + q, 16, patches) for p in range(3)]
        wide = jnp.concatenate([h, h, m, h, l, m], axis=0).astype(bf16)
        blank = jnp.zeros_like(wide)
        for k in range(2):
            rows2 = [wide if j == k else blank for j in range(2)]
            lfeat_ref[q, :, k * wpoints : (k + 1) * wpoints] = jnp.concatenate(rows2, axis=0)
        h, m, l = [get_wide(gw_ref, wtiles, p * 8 * patches + q, 8, patches) for p in range(3)]
        wide = jnp.concatenate([h, h, m, h, l, m], axis=0).astype(bf16)
        blank = jnp.zeros_like(wide)
        for k in range(shape.near):
            rows2 = [wide if j == k else blank for j in range(shape.near)]
            wfeat_ref[q, :, k * wpoints : (k + 1) * wpoints] = jnp.concatenate(rows2, axis=0)

    def wall_sources(b, y, n, v, w):
        w = -layer_scale * w
        v = [w * value for value in v]
        zero = jnp.zeros_like(w)
        ones = jnp.ones_like(w)
        square = y[0] * y[0] + y[1] * y[1] + y[2] * y[2] + soften
        dist = [-2.0 * y[0], -2.0 * y[1], -2.0 * y[2], square, ones, ones, ones]
        a = y[0] * v[0] + y[1] * v[1] + y[2] * v[2]
        c = y[0] * n[0] + y[1] * n[1] + y[2] * n[2]
        quad = [-(v[i] * c + n[i] * a) for i in range(3)] + [a * c]
        quad += [v[i] * n[i] for i in range(3)]
        quad += [v[i] * n[j] + v[j] * n[i] for i, j in ((0, 1), (0, 2), (1, 2))]
        for values, ref in ((dist, gd_ref), (quad, gq_ref)):
            for r, value in enumerate(values):
                for p, piece in enumerate(pieces(value)):
                    put_wide(ref, (16 * p + r) * patches, piece)
        for r, value in enumerate(y + [ones]):
            for p, piece in enumerate(pieces(value)):
                if p == 0 or r < 3:
                    put_wide(gm_ref, (4 * p + r) * patches, piece)

        def one_patch(q, _):
            slot = b * patches + q
            for k in range(wtiles):
                groups = []
                for ref in (gd_ref, gq_ref):
                    h, m, l = [
                        get_tile(ref, wtiles, k, p * 16 * patches + q, 16, patches) for p in range(3)
                    ]
                    groups += [h, m, h, l, h, m]
                block = jnp.concatenate(groups, axis=0).T.astype(bf16)
                lside_ref[slot, k * LANES : (k + 1) * LANES, :] = block
            rows16 = get_wide(gm_ref, wtiles, q, 16, patches)
            lmom_ref[slot] = rows16.astype(bf16)
            return 0

        lax.fori_loop(0, patches, one_patch, 0, unroll=2)

    wall_sources(
        1, x, [wnormal_ref[i] for i in range(3)], [wdensity_ref[i] for i in range(3)], wweight_ref[...]
    )

    for copy in weights:
        copy.wait()

    def membrane(first, count):
        tiles = [strided(e_ref, first * sub + k, count, sub) for k in range(sub)]
        value = jnp.concatenate(tiles, axis=1)
        centred = (value - jnp.mean(value, axis=1, keepdims=True)).astype(bf16)
        coeff = jnp.dot(centred, analysis_ref[...], preferred_element_type=f32)
        scaled = (coeff * stiffness_ref[...]).astype(bf16)
        force = -jnp.dot(scaled, synthesis_ref[...], preferred_element_type=f32)
        for k in range(sub):
            f_ref[pl.ds(first * sub + k, count, stride=sub), :] = force[:, k * LANES : (k + 1) * LANES]

    membrane(0, 3 * rows * cols)

    for copy in ws:
        copy.wait_recv()
    for b in range(2):
        wall_sources(
            2 * b,
            [hp_ref[b, i] for i in range(3)],
            [hn_ref[b, i] for i in range(3)],
            [hd_ref[b, i] for i in range(3)],
            hw_ref[b],
        )

    def pass_on(pairs):
        for copy, row in pairs:
            copy.wait_recv()
            for onward in sideways(row):
                onward.start()
                ys.append(onward)

    all_patches = patches * size_x * size_y
    block_start = (me_x * size_y + me_y) * patches

    def put_patch(ref, t, value):
        height = ref.shape[0] // wtiles
        for k in range(wtiles):
            at = pl.multiple_of(k * height + t * value.shape[0], 8)
            ref[pl.ds(at, value.shape[0]), :] = value[:, k * LANES : (k + 1) * LANES]

    def layer_slot(t, n):
        if n == 0:
            return t + patches
        slot = pnear_ref[n - 1, t] - block_start + patches
        slot = jnp.where(slot < 0, slot + all_patches, slot)
        slot = jnp.where(slot >= all_patches, slot - all_patches, slot)
        return jnp.clip(slot, 0, 3 * patches - 1)

    def layer_pair(j, _):
        slots = [[layer_slot(2 * j + u, n) for n in range(listed + 1)] for u in range(2)]
        scalars = []
        for u in range(2):
            side = jnp.concatenate([lside_ref[slot] for slot in slots[u]], axis=0)
            both = jnp.dot(side, lfeat_ref[2 * j + u], preferred_element_type=f32)
            root = lax.rsqrt(both[:, :wpoints])
            square = root * root
            scalars.append((both[:, wpoints:] * (square * square * root)).astype(bf16))
        moment = jnp.concatenate(
            [jnp.concatenate([lmom_ref[slot] for slot in slots[u]], axis=1) for u in range(2)], axis=0
        )
        total = jnp.dot(moment, jnp.concatenate(scalars, axis=1), preferred_element_type=f32)
        for u in range(2):
            put_patch(lacc_ref, 2 * j + u, total[16 * u : 16 * u + 16, u * wpoints : (u + 1) * wpoints])
        return 0

    done = 0
    for j in range(HALO):
        pass_on(xs[2 * j : 2 * j + 2])
        upto = patches // 2 if j == HALO - 1 else (j + 1) * patches // 8
        lax.fori_loop(done, upto, layer_pair, 0)
        done = upto

    membrane(3 * rows * cols, 3 * 2 * HALO * cols)
    for copy in ys:
        copy.wait_recv()
    membrane(3 * shape.left, -(-3 * (shape.slots - shape.left) // 8) * 8)

    def prepare(gids, side_ref, coef_ref, gs, gc):
        slots = [cell_slot(shape, gid, me_x, me_y) for gid in gids]
        sources = [(cell_points(e_cells, k, shape), cell_points(f_cells, k, shape)) for k in slots]
        prepare_sources(sources, side_ref, coef_ref, gs, gc, shape)

    def cell_prepare(i):
        r = lax.div(i, jnp.int32(cols))
        c = i - r * cols
        gids = [near_ref[r, n, c] for n in range(shape.near)]
        prepare(gids, side_ref, coef_ref, gs, gc)

    chunks = shape.points // WIDTH
    half = shape.near * 48
    parts = []
    for at in range(0, shape.points, WIDTH):
        for n in range(shape.near):
            parts.append((slice(at, at + WIDTH), n, slice(n * shape.points + at, n * shape.points + at + WIDTH)))

    def weigh(part, cube_ref):
        return jnp.dot(coef_ref[:, part], cube_ref[part, :], preferred_element_type=f32)

    def keep(t, acc):
        for k in range(WIDTH // LANES):
            tile = t * (WIDTH // LANES) + k
            h_ref[pl.ds(tile, acc.shape[0], stride=sub), :] = acc[:, k * LANES : (k + 1) * LANES]

    def cell_sums(i):
        for t in range(chunks):
            acc = None
            for near_rows, n, part in parts:
                first = (shape.near - 1 - n) * 48
                feat = feats_ref[i, first : first + half, t * WIDTH : (t + 1) * WIDTH]
                root = lax.rsqrt(jnp.dot(side_ref[near_rows, :], feat, preferred_element_type=f32))
                cubes[t % 2][part, :] = (root * root * root).astype(bf16)
                if t > 0:
                    more = weigh(part, cubes[(t - 1) % 2])
                    acc = more if acc is None else acc + more
            if t > 0:
                keep(t - 1, acc)
        acc = None
        for _, _, part in parts:
            more = weigh(part, cubes[(chunks - 1) % 2])
            acc = more if acc is None else acc + more
        keep(chunks - 1, acc)

    def cell_finish(i, best):
        r = lax.div(i, jnp.int32(cols))
        c = i - r * cols
        x = cell_points(e_cells, i, shape)

        def total(row):
            a, b, d = [h_ref[(p * COEF + row) * sub : (p * COEF + row + 1) * sub, :] for p in range(3)]
            return a + (b + d)

        parts = finish(x, total)
        own = cell_points(f_cells, i, shape)
        drag = drag_ref[r, c]
        squared = jnp.zeros_like(best)
        values = []
        for k in range(3):
            value = drag * own[k] + parts[k]
            values.append(value)
            squared = squared + value * value
        v_ref[pl.ds(pl.multiple_of(i * cell, 8), cell), :] = jnp.concatenate(values, axis=0)
        return jnp.maximum(best, squared)

    def cell_step(i, best):
        cell_sums(i)
        cell_prepare(jnp.minimum(i + 1, rows * cols - 1))
        return cell_finish(i, best)

    cell_prepare(jnp.int32(0))
    best = lax.fori_loop(0, rows * cols, cell_step, jnp.zeros((sub, LANES), f32))
    mine_ref[...] = best

    sets = ((side_ref, coef_ref, gs, gc), (side_b, coef_b, (gs_c, gs_d), (gc_c, gc_d)))

    def wall_prepare(j):
        for u in range(2):
            gids = [cpatch_ref[n, 2 * j + u] for n in range(shape.near)]
            prepare(gids, *sets[u])

    def wall_pair(j, _):
        accs = [None, None]
        for at in range(0, shape.points, WIDTH):
            cubes2 = []
            for u in range(2):
                square = jnp.dot(
                    sets[u][0][at : at + WIDTH, :], wfeat_ref[2 * j + u], preferred_element_type=f32
                )
                root = lax.rsqrt(square)
                cubes2.append((root * root * root).astype(bf16))
            for u in range(2):
                coef = sets[u][1]
                both = jnp.concatenate(
                    [coef[:, n * shape.points + at : n * shape.points + at + WIDTH] for n in range(shape.near)],
                    axis=0,
                )
                more = jnp.dot(both, cubes2[u], preferred_element_type=f32)
                accs[u] = more if accs[u] is None else accs[u] + more
        count = coef_ref.shape[0]
        for u in range(2):
            blocks = [
                accs[u][n * count : (n + 1) * count, n * wpoints : (n + 1) * wpoints]
                for n in range(shape.near)
            ]
            put_patch(wacc_ref, 2 * j + u, functools.reduce(jnp.add, blocks))
        wall_prepare(jnp.minimum(j + 1, patches // 2 - 1))
        return 0

    wall_prepare(jnp.int32(0))
    copies = []
    for d, device in enumerate(peers_y):
        copies.append(remote(mine_ref, from_y.at[d], tsend_y.at[d], trecv_y.at[d], device))
        copies[-1].start()
    lax.fori_loop(0, 1, wall_pair, 0)
    best = mine_ref[...]
    for d, copy in enumerate(copies):
        copy.wait_recv()
        best = jnp.maximum(best, from_y[d])
    row_ref[...] = best
    moment = [get_wide(lacc_ref, wtiles, r, patches, 16) for r in range(11)]
    moment = [moment[i] + (moment[4 + i] + moment[8 + i]) for i in range(3)] + [moment[3]]
    for i in range(3):
        half_ref[i] = x[i] * moment[3] - moment[i]
    for d, device in enumerate(peers_x):
        copies.append(remote(row_ref, from_x.at[d], tsend_x.at[d], trecv_x.at[d], device))
        copies[-1].start()
    lax.fori_loop(1, patches // 2, wall_pair, 0)

    def wall_total(row):
        a, b, d = [
            get_wide(wacc_ref, wtiles, p * COEF + row, patches, coef_ref.shape[0]) for p in range(3)
        ]
        return a + (b + d)

    flow = finish(x, wall_total)
    for i in range(3):
        half_ref[i] = half_ref[i] + flow[i]

    best = row_ref[...]
    for d, copy in enumerate(copies[size_y - 1 :]):
        copy.wait_recv()
        best = jnp.maximum(best, from_x[d])
    top_ref[...] = best
    for r in range(rows):
        for c in range(cols):
            for i in range(3):
                at = ((r * cols + c) * 3 + i) * sub
                speed_ref[pl.ds((r * 3 + i) * sub * cols + c, sub, stride=cols), :] = v_ref[at : at + sub, :]
    for copy, _ in xs:
        copy.wait_send()
    for copy in ws + ys + copies:
        copy.wait_send()


def update_kernel(pos_ref, speed_ref, top_ref, half_ref, moved_ref, dens_ref):
    top = jnp.sqrt(jnp.max(top_ref[...], keepdims=True))
    step = 1.0 / (top + 1e-06)
    moved_ref[...] = pos_ref[...] + step * speed_ref[...]
    dens_ref[...] = 2.0 * half_ref[...]


def body(
    cell_pos,
    cell_drag,
    cell_near,
    analysis,
    stiffness,
    synthesis,
    wall_pos,
    wall_normal,
    wall_weight,
    density,
    patch_near,
    cell_to_patch,
):
    rows, cols, _, points = cell_pos.shape
    size_x, size_y = lax.axis_size("cx"), lax.axis_size("cy")
    near = cell_near.shape[2]
    listed = patch_near.shape[1]
    patches, _, wpoints = wall_pos.shape
    shape = Shape(rows, cols, points, size_x, size_y, near)
    sub, cell = shape.sub, shape.cell
    raw = cell_pos.reshape(rows, cols, 3, sub, LANES)
    raw = jnp.transpose(raw, (0, 2, 3, 1, 4)).reshape(rows * 3 * sub * cols, LANES)
    wtiles = wpoints // LANES
    spare = -(-shape.slots // 8) * 8
    sources = near * points
    assert cell_to_patch.shape[1] == near and patches % 2 == 0
    coef_rows = -(-3 * COEF // 16) * 16
    dma = pltpu.SemaphoreType.DMA
    vmem = pltpu.VMEM
    in_vmem = pl.BlockSpec(memory_space=pltpu.VMEM)
    in_smem = pl.BlockSpec(memory_space=pltpu.SMEM)
    in_hbm = pl.BlockSpec(memory_space=pltpu.HBM)
    walls = lambda v: jnp.transpose(v, (1, 0, 2))
    speed, top, half = pl.pallas_call(
        functools.partial(mega_kernel, shape, listed),
        out_shape=(
            jax.ShapeDtypeStruct(raw.shape, f32),
            jax.ShapeDtypeStruct((sub, LANES), f32),
            jax.ShapeDtypeStruct((3, patches, wpoints), f32),
        ),
        in_specs=[
            in_smem, in_smem, in_hbm, in_hbm, in_hbm, in_hbm,
            in_hbm, in_hbm, in_hbm, in_hbm, in_smem, in_smem,
        ],
        out_specs=[in_vmem] * 3,
        scratch_shapes=[
            vmem(raw.shape, f32),
            vmem((1, stiffness.shape[0]), f32),
            vmem((3, patches, wpoints), f32),
            vmem((3, patches, wpoints), f32),
            vmem((patches, wpoints), f32),
            vmem((3, patches, wpoints), f32),
            vmem(analysis.shape, bf16),
            vmem(synthesis.shape, bf16),
            vmem((spare, cell, LANES), f32),
            vmem((spare, cell, LANES), f32),
            vmem((rows * cols * cell, LANES), f32),
            vmem((24 * sub, LANES), f32),
            vmem((24 * sub, LANES), f32),
            vmem((24 * sub, LANES), f32),
            vmem((24 * sub, LANES), f32),
            vmem((coef_rows * sub, LANES), f32),
            vmem((coef_rows * sub, LANES), f32),
            vmem((coef_rows * sub, LANES), f32),
            vmem((coef_rows * sub, LANES), f32),
            vmem((24 * sub, LANES), f32),
            vmem((points, near * 48), bf16),
            vmem((coef_rows, sources), bf16),
            vmem((points, near * 48), bf16),
            vmem((coef_rows, sources), bf16),
            vmem((rows * cols, (2 * near - 1) * 48, points), bf16),
            vmem((sources, WIDTH), bf16),
            vmem((sources, WIDTH), bf16),
            vmem((coef_rows * sub, LANES), f32),
            vmem((2, 3, patches, wpoints), f32),
            vmem((2, 3, patches, wpoints), f32),
            vmem((2, 3, patches, wpoints), f32),
            vmem((2, patches, wpoints), f32),
            vmem((48 * patches * wtiles, LANES), f32),
            vmem((48 * patches * wtiles, LANES), f32),
            vmem((16 * patches * wtiles, LANES), f32),
            vmem((48 * patches * wtiles, LANES), f32),
            vmem((24 * patches * wtiles, LANES), f32),
            vmem((3 * patches, wpoints, 192), bf16),
            vmem((3 * patches, 16, wpoints), bf16),
            vmem((patches, 192, 2 * wpoints), bf16),
            vmem((patches, near * 48, near * wpoints), bf16),
            vmem((patches * 16 * wtiles, LANES), f32),
            vmem((patches * coef_rows * wtiles, LANES), f32),
            vmem((sub, LANES), f32),
            vmem((sub, LANES), f32),
            vmem((size_y - 1, sub, LANES), f32),
            vmem((size_x - 1, sub, LANES), f32),
            dma((8,)),
            dma((2 * HALO,)),
            dma((2 * HALO,)),
            dma((2 * shape.ext_rows,)),
            dma((2 * shape.ext_rows,)),
            dma((8,)),
            dma((8,)),
            dma((size_y - 1,)),
            dma((size_y - 1,)),
            dma((size_x - 1,)),
            dma((size_x - 1,)),
        ],
        compiler_params=pltpu.CompilerParams(
            collective_id=0, has_side_effects=True, vmem_limit_bytes=62 * 2**20
        ),
        name="mega",
    )(
        jnp.transpose(cell_near, (0, 2, 1)),
        cell_drag,
        raw,
        analysis,
        stiffness[None, :],
        synthesis,
        walls(wall_pos),
        walls(wall_normal),
        wall_weight,
        walls(density),
        jnp.transpose(patch_near),
        jnp.transpose(cell_to_patch),
    )
    moved, dens = pl.pallas_call(
        update_kernel,
        out_shape=(
            jax.ShapeDtypeStruct(raw.shape, f32),
            jax.ShapeDtypeStruct((3, patches, wpoints), f32),
        ),
        in_specs=[in_vmem] * 4,
        out_specs=[in_vmem] * 2,
        name="update",
    )(raw, speed, top, half)
    moved = jnp.transpose(moved.reshape(rows, 3, sub, cols, LANES), (0, 3, 1, 2, 4))
    return moved.reshape(cell_pos.shape), jnp.transpose(dens, (1, 0, 2))


def solution(mesh):
    placed = (
        P("cx", "cy", None, None),
        P("cx", "cy"),
        P("cx", "cy", None),
        P(),
        P(),
        P(),
        P(("cx", "cy"), None, None),
        P(("cx", "cy"), None, None),
        P(("cx", "cy"), None),
        P(("cx", "cy"), None, None),
        P(("cx", "cy"), None),
        P(("cx", "cy"), None),
    )
    return jax.shard_map(
        body,
        mesh=mesh,
        in_specs=placed,
        out_specs=(P("cx", "cy", None, None), P(("cx", "cy"), None, None)),
        check_vma=False,
    )
```

```python
import functools
import math

import jax
import jax.numpy as jnp
from jax import lax
from jax.experimental import pallas as pl
from jax.experimental.pallas import tpu as pltpu
from jax.sharding import PartitionSpec as P

HALO = 3
LANES = 128
WIDTH = 512

soften = 0.25
stokes_scale = 1.0 / (8.0 * math.pi)
layer_scale = 3.0 / (4.0 * math.pi)

MESH = pl.DeviceIdType.MESH
f32 = jnp.float32
bf16 = jnp.bfloat16


def pieces(value):
    high = value.astype(bf16).astype(f32)
    rest = value - high
    middle = rest.astype(bf16).astype(f32)
    return high, middle, rest - middle


def strided(ref, start, count, stride):
    return ref[pl.ds(start, count, stride=stride), :]


def put_wide(ref, first, value):
    tiles = value.shape[1] // LANES
    height = ref.shape[0] // tiles
    for k in range(tiles):
        at = k * height + first
        ref[at : at + value.shape[0], :] = value[:, k * LANES : (k + 1) * LANES]


def get_tile(ref, tiles, tile, start, count, stride):
    height = ref.shape[0] // tiles
    return ref[pl.ds(tile * height + start, count, stride=stride), :]


def get_wide(ref, tiles, start, count, stride):
    return jnp.concatenate([get_tile(ref, tiles, k, start, count, stride) for k in range(tiles)], axis=1)


class Shape:
    def __init__(self, rows, cols, points, size_x, size_y, near):
        self.rows, self.cols, self.points = rows, cols, points
        self.size_x, self.size_y, self.near = size_x, size_y, near
        self.ext_rows = rows + 2 * HALO
        self.sub = points // LANES
        self.cell = 3 * self.sub
        self.left = self.ext_rows * cols
        self.right = self.left + self.ext_rows * HALO
        self.slots = self.right + self.ext_rows * HALO


def cell_slot(shape, gid, me_x, me_y):
    all_rows, all_cols = shape.rows * shape.size_x, shape.cols * shape.size_y
    grid_row = lax.div(gid, jnp.int32(all_cols))
    grid_col = gid - grid_row * all_cols
    row = grid_row - me_x * shape.rows
    row = jnp.where(row < 0, row + all_rows, row)
    row = jnp.where(row >= shape.rows + HALO, row - all_rows + shape.ext_rows, row)
    col = grid_col - me_y * shape.cols + HALO
    col = jnp.where(col < 0, col + all_cols, col)
    col = jnp.where(col >= all_cols, col - all_cols, col)
    middle = row * shape.cols + col - HALO
    left = shape.left + row * HALO + col
    right = shape.right + row * HALO + col - HALO - shape.cols
    slot = jnp.where(col < HALO, left, jnp.where(col >= HALO + shape.cols, right, middle))
    return jnp.clip(slot, 0, shape.slots - 1)


def cell_points(ref, slot, shape):
    block = ref[slot]
    return [block[i * shape.sub : (i + 1) * shape.sub] for i in range(3)]


def put_rows(ref, sub, first, values):
    for i, value in enumerate(values):
        ref[(first + i) * sub : (first + i + 1) * sub, :] = value


def prepare_sources(sources, side_ref, coef_ref, gs, gc, shape):
    sub, points = shape.sub, shape.points
    for n, (y, f) in enumerate(sources):
        square = y[0] * y[0] + y[1] * y[1] + y[2] * y[2]
        split = [pieces(v) for v in (-2.0 * y[0], -2.0 * y[1], -2.0 * y[2], square + soften)]
        for p in range(3):
            put_rows(gs[n], sub, 8 * p, [split[0][p], split[1][p], split[2][p]])
            put_rows(gs[n], sub, 8 * p + 4, [split[3][p]])
        along = y[0] * f[0] + y[1] * f[1] + y[2] * f[2]
        line = [f[0], f[1], f[2], along]
        values = list(line)
        for i in range(3):
            values += [y[i] * v for v in line]
        values += [square * v for v in f]
        for r, value in enumerate(values):
            for p, piece in enumerate(pieces(value)):
                put_rows(gc[n], sub, p * COEF + r, [piece])
    for k in range(sub):
        groups = []
        for n in range(len(sources)):
            h, m, l = [strided(gs[n], p * 8 * sub + k, 8, sub) for p in range(3)]
            groups += [h, m, h, l, h, m]
            rows = strided(gc[n], k, coef_ref.shape[0], sub)
            at = n * points + k * LANES
            coef_ref[:, at : at + LANES] = rows.astype(bf16)
        block = jnp.concatenate(groups, axis=0).T.astype(bf16)
        side_ref[k * LANES : (k + 1) * LANES, :] = block


COEF = 19


def finish(x, total):
    line = x[0] * total(0) + x[1] * total(1) + x[2] * total(2) - total(3)
    square = x[0] * x[0] + x[1] * x[1] + x[2] * x[2] + 2.0 * soften
    low = [total(i) for i in range(3)]
    near = [[total(4 + 4 * j + i) for i in range(4)] for j in range(3)]
    far = [total(16 + i) for i in range(3)]
    out = []
    for i in range(3):
        cross = x[0] * near[0][i] + x[1] * near[1][i] + x[2] * near[2][i]
        turned = x[0] * near[i][0] + x[1] * near[i][1] + x[2] * near[i][2] - near[i][3]
        direct = square * low[i] + far[i] - 2.0 * cross
        out.append(stokes_scale * (direct + x[i] * line - turned))
    return out


def mega_kernel(
    shape,
    listed,
    near_ref,
    drag_ref,
    pos_hbm,
    analysis_hbm,
    stiffness_hbm,
    synthesis_hbm,
    wpos_hbm,
    wnormal_hbm,
    wweight_hbm,
    wdensity_hbm,
    pnear_ref,
    cpatch_ref,
    speed_ref,
    top_ref,
    half_ref,
    pos_ref,
    stiffness_ref,
    wpos_ref,
    wnormal_ref,
    wweight_ref,
    wdensity_ref,
    analysis_ref,
    synthesis_ref,
    e_ref,
    f_ref,
    v_ref,
    gs_a,
    gs_b,
    gs_c,
    gs_d,
    gc_a,
    gc_b,
    gc_c,
    gc_d,
    gt_ref,
    side_ref,
    coef_ref,
    side_b,
    coef_b,
    feats_ref,
    cube_a,
    cube_b,
    h_ref,
    hp_ref,
    hn_ref,
    hd_ref,
    hw_ref,
    gd_ref,
    gq_ref,
    gm_ref,
    gf_ref,
    gw_ref,
    lside_ref,
    lmom_ref,
    lfeat_ref,
    wfeat_ref,
    lacc_ref,
    wacc_ref,
    mine_ref,
    row_ref,
    from_y,
    from_x,
    local,
    xsend,
    xrecv,
    ysend,
    yrecv,
    wsend,
    wrecv,
    tsend_y,
    trecv_y,
    tsend_x,
    trecv_x,
):
    me_x, me_y = lax.axis_index("cx"), lax.axis_index("cy")
    e_cells, f_cells = e_ref, f_ref
    e_ref = e_cells.reshape(e_cells.shape[0] * e_cells.shape[1], LANES)
    f_ref = f_cells.reshape(f_cells.shape[0] * f_cells.shape[1], LANES)
    gs, gc, cubes = (gs_a, gs_b), (gc_a, gc_b), (cube_a, cube_b)
    size_x, size_y = shape.size_x, shape.size_y
    rows, cols, sub, cell = shape.rows, shape.cols, shape.sub, shape.cell
    patches, wpoints = wpos_hbm.shape[1], wpos_hbm.shape[2]
    wtiles = wpoints // LANES

    weights = [
        pltpu.make_async_copy(analysis_hbm, analysis_ref, local.at[0]),
        pltpu.make_async_copy(synthesis_hbm, synthesis_ref, local.at[1]),
        pltpu.make_async_copy(stiffness_hbm, stiffness_ref, local.at[2]),
    ]
    pairs = (
        (pos_hbm, pos_ref), (wpos_hbm, wpos_ref), (wnormal_hbm, wnormal_ref),
        (wweight_hbm, wweight_ref), (wdensity_hbm, wdensity_ref),
    )
    inputs = [pltpu.make_async_copy(src, dst, local.at[3 + k]) for k, (src, dst) in enumerate(pairs)]
    for copy in inputs + weights:
        copy.start()

    def around(step_x, step_y):
        return (lax.rem(me_x + step_x + size_x, size_x), lax.rem(me_y + step_y + size_y, size_y))

    def along_walls(step):
        other = lax.rem(me_x * size_y + me_y + step + size_x * size_y, size_x * size_y)
        there = lax.div(other, jnp.int32(size_y))
        return (there, other - there * size_y)

    peers_y = [around(0, d) for d in range(1, size_y)]
    peers_x = [around(d, 0) for d in range(1, size_x)]
    after, before = along_walls(1), along_walls(-1)
    greeted = peers_y + peers_x + [after, before]
    barrier = pltpu.get_barrier_semaphore()
    for device in greeted:
        pl.semaphore_signal(barrier, inc=1, device_id=device, device_id_type=MESH)

    e_ref[shape.slots * cell :, :] = jnp.zeros_like(e_ref[shape.slots * cell :, :])
    for ref in (*gs, gs_c, gs_d, *gc, gc_c, gc_d, gt_ref, gd_ref, gq_ref, gm_ref, gf_ref, gw_ref):
        ref[...] = jnp.zeros_like(ref)
    one = jnp.ones((sub, LANES), f32)
    for ref in (*gs, gs_c, gs_d):
        ref[3 * sub : 4 * sub, :] = one
    gt_ref[4 * sub : 5 * sub, :] = one
    for copy in inputs:
        copy.wait()
    for r in range(rows):
        for c in range(cols):
            for i in range(3):
                at = ((r * cols + c) * 3 + i) * sub
                e_ref[at : at + sub, :] = strided(pos_ref, (r * 3 + i) * sub * cols + c, sub, cols)

    pl.semaphore_wait(barrier, len(greeted))

    def remote(src, dst, send, recv, device):
        return pltpu.make_async_remote_copy(
            src_ref=src,
            dst_ref=dst,
            send_sem=send,
            recv_sem=recv,
            device_id=device,
            device_id_type=MESH,
        )

    def cells(slot, count):
        return e_cells.at[slot : slot + count]

    xs = []
    for j in range(HALO):
        k = 2 * j
        up = remote(
            cells((rows - HALO + j) * cols, cols),
            cells((rows + HALO + j) * cols, cols),
            xsend.at[k], xrecv.at[k], around(1, 0),
        )
        down = remote(
            cells(j * cols, cols), cells((rows + j) * cols, cols),
            xsend.at[k + 1], xrecv.at[k + 1], around(-1, 0),
        )
        xs += [(up, rows + HALO + j), (down, rows + j)]

    def sideways(row):
        right = remote(
            cells(row * cols + cols - HALO, HALO), cells(shape.left + row * HALO, HALO),
            ysend.at[2 * row], yrecv.at[2 * row], around(0, 1),
        )
        left = remote(
            cells(row * cols, HALO), cells(shape.right + row * HALO, HALO),
            ysend.at[2 * row + 1], yrecv.at[2 * row + 1], around(0, -1),
        )
        return [right, left]

    ws = []
    sources = ((wpos_ref, hp_ref), (wnormal_ref, hn_ref), (wdensity_ref, hd_ref), (wweight_ref, hw_ref))
    for b, device in enumerate((after, before)):
        for src, dst in sources:
            k = len(ws)
            ws.append(remote(src, dst.at[b], wsend.at[k], wrecv.at[k], device))

    for copy in ws:
        copy.start()
    for copy, _ in xs:
        copy.start()
    ys = []
    for row in range(rows):
        for copy in sideways(row):
            copy.start()
            ys.append(copy)

    def target(i, _):
        x = cell_points(e_cells, i, shape)
        square = x[0] * x[0] + x[1] * x[1] + x[2] * x[2]
        split = [pieces(v) for v in (x[0], x[1], x[2], square)]
        for p in range(3):
            put_rows(gt_ref, sub, 8 * p, [s[p] for s in split])
        tiles = []
        for k in range(sub):
            h, m, l = [strided(gt_ref, p * 8 * sub + k, 8, sub) for p in range(3)]
            tiles.append(jnp.concatenate([h, h, m, h, l, m], axis=0).astype(bf16))
        first = (shape.near - 1) * 48
        blank = jnp.zeros((first, shape.points), bf16)
        feats_ref[i, :first, :] = blank
        feats_ref[i, first : first + 48, :] = jnp.concatenate(tiles, axis=1)
        feats_ref[i, first + 48 :, :] = blank
        return 0

    lax.fori_loop(0, rows * cols, target, 0)

    x = [wpos_ref[i] for i in range(3)]
    lone = jnp.ones((patches, wpoints), f32)
    squares = [x[i] * x[i] for i in range(3)]
    mono = x + [lone] + squares + [x[0] * x[1], x[0] * x[2], x[1] * x[2]]
    square = squares[0] + squares[1] + squares[2]
    for r, value in enumerate(mono):
        for p, piece in enumerate(pieces(value)):
            put_wide(gf_ref, (16 * p + r) * patches, piece)
    for r, value in enumerate(x + [square, lone]):
        for p, piece in enumerate(pieces(value)):
            put_wide(gw_ref, (8 * p + r) * patches, piece)
    for q in range(patches):
        h, m, l = [get_wide(gf_ref, wtiles, p * 16 * patches + q, 16, patches) for p in range(3)]
        wide = jnp.concatenate([h, h, m, h, l, m], axis=0).astype(bf16)
        blank = jnp.zeros_like(wide)
        for k in range(2):
            rows2 = [wide if j == k else blank for j in range(2)]
            lfeat_ref[q, :, k * wpoints : (k + 1) * wpoints] = jnp.concatenate(rows2, axis=0)
        h, m, l = [get_wide(gw_ref, wtiles, p * 8 * patches + q, 8, patches) for p in range(3)]
        wide = jnp.concatenate([h, h, m, h, l, m], axis=0).astype(bf16)
        blank = jnp.zeros_like(wide)
        for k in range(shape.near):
            rows2 = [wide if j == k else blank for j in range(shape.near)]
            wfeat_ref[q, :, k * wpoints : (k + 1) * wpoints] = jnp.concatenate(rows2, axis=0)

    def wall_sources(b, y, n, v, w):
        w = -layer_scale * w
        v = [w * value for value in v]
        zero = jnp.zeros_like(w)
        ones = jnp.ones_like(w)
        square = y[0] * y[0] + y[1] * y[1] + y[2] * y[2] + soften
        dist = [-2.0 * y[0], -2.0 * y[1], -2.0 * y[2], square, ones, ones, ones]
        a = y[0] * v[0] + y[1] * v[1] + y[2] * v[2]
        c = y[0] * n[0] + y[1] * n[1] + y[2] * n[2]
        quad = [-(v[i] * c + n[i] * a) for i in range(3)] + [a * c]
        quad += [v[i] * n[i] for i in range(3)]
        quad += [v[i] * n[j] + v[j] * n[i] for i, j in ((0, 1), (0, 2), (1, 2))]
        for values, ref in ((dist, gd_ref), (quad, gq_ref)):
            for r, value in enumerate(values):
                for p, piece in enumerate(pieces(value)):
                    put_wide(ref, (16 * p + r) * patches, piece)
        for r, value in enumerate(y + [ones]):
            for p, piece in enumerate(pieces(value)):
                if p == 0 or r < 3:
                    put_wide(gm_ref, (4 * p + r) * patches, piece)

        def one_patch(q, _):
            slot = b * patches + q
            for k in range(wtiles):
                groups = []
                for ref in (gd_ref, gq_ref):
                    h, m, l = [
                        get_tile(ref, wtiles, k, p * 16 * patches + q, 16, patches) for p in range(3)
                    ]
                    groups += [h, m, h, l, h, m]
                block = jnp.concatenate(groups, axis=0).T.astype(bf16)
                lside_ref[slot, k * LANES : (k + 1) * LANES, :] = block
            rows16 = get_wide(gm_ref, wtiles, q, 16, patches)
            lmom_ref[slot] = rows16.astype(bf16)
            return 0

        lax.fori_loop(0, patches, one_patch, 0, unroll=2)

    wall_sources(
        1, x, [wnormal_ref[i] for i in range(3)], [wdensity_ref[i] for i in range(3)], wweight_ref[...]
    )

    for copy in weights:
        copy.wait()

    def membrane(first, count):
        tiles = [strided(e_ref, first * sub + k, count, sub) for k in range(sub)]
        value = jnp.concatenate(tiles, axis=1)
        centred = (value - jnp.mean(value, axis=1, keepdims=True)).astype(bf16)
        coeff = jnp.dot(centred, analysis_ref[...], preferred_element_type=f32)
        scaled = (coeff * stiffness_ref[...]).astype(bf16)
        force = -jnp.dot(scaled, synthesis_ref[...], preferred_element_type=f32)
        for k in range(sub):
            f_ref[pl.ds(first * sub + k, count, stride=sub), :] = force[:, k * LANES : (k + 1) * LANES]

    membrane(0, 3 * rows * cols)

    def pass_on(pairs):
        for copy, row in pairs:
            copy.wait_recv()
            for onward in sideways(row):
                onward.start()
                ys.append(onward)

    all_patches = patches * size_x * size_y
    block_start = (me_x * size_y + me_y) * patches

    def put_patch(ref, t, value):
        height = ref.shape[0] // wtiles
        for k in range(wtiles):
            at = pl.multiple_of(k * height + t * value.shape[0], 8)
            ref[pl.ds(at, value.shape[0]), :] = value[:, k * LANES : (k + 1) * LANES]

    def layer_slot(t, n):
        if n == 0:
            return t + patches
        slot = pnear_ref[n - 1, t] - block_start + patches
        slot = jnp.where(slot < 0, slot + all_patches, slot)
        slot = jnp.where(slot >= all_patches, slot - all_patches, slot)
        return jnp.clip(slot, 0, 3 * patches - 1)

    def layer_pair(j, _):
        slots = [[layer_slot(2 * j + u, n) for n in range(listed + 1)] for u in range(2)]
        scalars = []
        for u in range(2):
            side = jnp.concatenate([lside_ref[slot] for slot in slots[u]], axis=0)
            both = jnp.dot(side, lfeat_ref[2 * j + u], preferred_element_type=f32)
            root = lax.rsqrt(both[:, :wpoints])
            square = root * root
            scalars.append((both[:, wpoints:] * (square * square * root)).astype(bf16))
        moment = jnp.concatenate(
            [jnp.concatenate([lmom_ref[slot] for slot in slots[u]], axis=1) for u in range(2)], axis=0
        )
        total = jnp.dot(moment, jnp.concatenate(scalars, axis=1), preferred_element_type=f32)
        for u in range(2):
            put_patch(lacc_ref, 2 * j + u, total[16 * u : 16 * u + 16, u * wpoints : (u + 1) * wpoints])
        return 0

    pass_on(xs[:1])
    for copy in ws:
        copy.wait_recv()
    for b in range(1):
        wall_sources(
            2 * b,
            [hp_ref[b, i] for i in range(3)],
            [hn_ref[b, i] for i in range(3)],
            [hd_ref[b, i] for i in range(3)],
            hw_ref[b],
        )

    pass_on(xs[1:2])
    for b in range(1, 2):
        wall_sources(
            2 * b,
            [hp_ref[b, i] for i in range(3)],
            [hn_ref[b, i] for i in range(3)],
            [hd_ref[b, i] for i in range(3)],
            hw_ref[b],
        )

    pass_on(xs[2:4])
    lax.fori_loop(0, 1, layer_pair, 0)
    pass_on(xs[4:5])
    lax.fori_loop(1, 2, layer_pair, 0)
    pass_on(xs[5:])
    lax.fori_loop(2, patches // 2, layer_pair, 0)

    membrane(3 * rows * cols, 3 * 2 * HALO * cols)
    for copy in ys:
        copy.wait_recv()
    membrane(3 * shape.left, -(-3 * (shape.slots - shape.left) // 8) * 8)

    def prepare(gids, side_ref, coef_ref, gs, gc):
        slots = [cell_slot(shape, gid, me_x, me_y) for gid in gids]
        sources = [(cell_points(e_cells, k, shape), cell_points(f_cells, k, shape)) for k in slots]
        prepare_sources(sources, side_ref, coef_ref, gs, gc, shape)

    def cell_prepare(i):
        r = lax.div(i, jnp.int32(cols))
        c = i - r * cols
        gids = [near_ref[r, n, c] for n in range(shape.near)]
        prepare(gids, side_ref, coef_ref, gs, gc)

    chunks = shape.points // WIDTH
    half = shape.near * 48
    parts = []
    for n in range(shape.near):
        parts.append((slice(0, shape.points), n, slice(n * shape.points, (n + 1) * shape.points)))

    def weigh(part, cube_ref):
        return jnp.dot(coef_ref[:, part], cube_ref[part, :], preferred_element_type=f32)

    def keep(t, acc):
        for k in range(WIDTH // LANES):
            tile = t * (WIDTH // LANES) + k
            h_ref[pl.ds(tile, acc.shape[0], stride=sub), :] = acc[:, k * LANES : (k + 1) * LANES]

    def cell_sums(i):
        for t in range(chunks):
            acc = None
            for near_rows, n, part in parts:
                first = (shape.near - 1 - n) * 48
                feat = feats_ref[i, first : first + half, t * WIDTH : (t + 1) * WIDTH]
                root = lax.rsqrt(jnp.dot(side_ref[near_rows, :], feat, preferred_element_type=f32))
                cubes[t % 2][part, :] = (root * root * root).astype(bf16)
                if t > 0:
                    more = weigh(part, cubes[(t - 1) % 2])
                    acc = more if acc is None else acc + more
            if t > 0:
                keep(t - 1, acc)
        acc = None
        for _, _, part in parts:
            more = weigh(part, cubes[(chunks - 1) % 2])
            acc = more if acc is None else acc + more
        keep(chunks - 1, acc)

    def cell_finish(i, best):
        r = lax.div(i, jnp.int32(cols))
        c = i - r * cols
        x = cell_points(e_cells, i, shape)

        def total(row):
            a, b, d = [h_ref[(p * COEF + row) * sub : (p * COEF + row + 1) * sub, :] for p in range(3)]
            return a + (b + d)

        parts = finish(x, total)
        own = cell_points(f_cells, i, shape)
        drag = drag_ref[r, c]
        squared = jnp.zeros_like(best)
        values = []
        for k in range(3):
            value = drag * own[k] + parts[k]
            values.append(value)
            squared = squared + value * value
        v_ref[pl.ds(pl.multiple_of(i * cell, 8), cell), :] = jnp.concatenate(values, axis=0)
        return jnp.maximum(best, squared)

    def cell_step(i, best):
        cell_sums(i)
        cell_prepare(jnp.minimum(i + 1, rows * cols - 1))
        return cell_finish(i, best)

    cell_prepare(jnp.int32(0))
    best = lax.fori_loop(0, rows * cols, cell_step, jnp.zeros((sub, LANES), f32))
    mine_ref[...] = best

    sets = ((side_ref, coef_ref, gs, gc), (side_b, coef_b, (gs_c, gs_d), (gc_c, gc_d)))

    def wall_prepare(j):
        for u in range(2):
            gids = [cpatch_ref[n, 2 * j + u] for n in range(shape.near)]
            prepare(gids, *sets[u])

    def wall_pair(j, _):
        accs = [None, None]
        for at in range(0, shape.points, WIDTH):
            cubes2 = []
            for u in range(2):
                square = jnp.dot(
                    sets[u][0][at : at + WIDTH, :], wfeat_ref[2 * j + u], preferred_element_type=f32
                )
                root = lax.rsqrt(square)
                cubes2.append((root * root * root).astype(bf16))
            for u in range(2):
                coef = sets[u][1]
                both = jnp.concatenate(
                    [coef[:, n * shape.points + at : n * shape.points + at + WIDTH] for n in range(shape.near)],
                    axis=0,
                )
                more = jnp.dot(both, cubes2[u], preferred_element_type=f32)
                accs[u] = more if accs[u] is None else accs[u] + more
        count = coef_ref.shape[0]
        for u in range(2):
            blocks = [
                accs[u][n * count : (n + 1) * count, n * wpoints : (n + 1) * wpoints]
                for n in range(shape.near)
            ]
            put_patch(wacc_ref, 2 * j + u, functools.reduce(jnp.add, blocks))
        wall_prepare(jnp.minimum(j + 1, patches // 2 - 1))
        return 0

    wall_prepare(jnp.int32(0))
    copies = []
    for d, device in enumerate(peers_y):
        copies.append(remote(mine_ref, from_y.at[d], tsend_y.at[d], trecv_y.at[d], device))
        copies[-1].start()
    lax.fori_loop(0, 1, wall_pair, 0)
    best = mine_ref[...]
    for d, copy in enumerate(copies):
        copy.wait_recv()
        best = jnp.maximum(best, from_y[d])
    row_ref[...] = best
    moment = [get_wide(lacc_ref, wtiles, r, patches, 16) for r in range(11)]
    moment = [moment[i] + (moment[4 + i] + moment[8 + i]) for i in range(3)] + [moment[3]]
    for i in range(3):
        half_ref[i] = x[i] * moment[3] - moment[i]
    for d, device in enumerate(peers_x):
        copies.append(remote(row_ref, from_x.at[d], tsend_x.at[d], trecv_x.at[d], device))
        copies[-1].start()
    lax.fori_loop(1, patches // 2, wall_pair, 0)

    def wall_total(row):
        a, b, d = [
            get_wide(wacc_ref, wtiles, p * COEF + row, patches, coef_ref.shape[0]) for p in range(3)
        ]
        return a + (b + d)

    flow = finish(x, wall_total)
    for i in range(3):
        half_ref[i] = half_ref[i] + flow[i]

    best = row_ref[...]
    for d, copy in enumerate(copies[size_y - 1 :]):
        copy.wait_recv()
        best = jnp.maximum(best, from_x[d])
    top_ref[...] = best
    for r in range(rows):
        for c in range(cols):
            for i in range(3):
                at = ((r * cols + c) * 3 + i) * sub
                speed_ref[pl.ds((r * 3 + i) * sub * cols + c, sub, stride=cols), :] = v_ref[at : at + sub, :]
    for copy, _ in xs:
        copy.wait_send()
    for copy in ws + ys + copies:
        copy.wait_send()


def update_kernel(pos_ref, speed_ref, top_ref, half_ref, moved_ref, dens_ref):
    top = jnp.sqrt(jnp.max(top_ref[...], keepdims=True))
    step = 1.0 / (top + 1e-06)
    moved_ref[...] = pos_ref[...] + step * speed_ref[...]
    dens_ref[...] = 2.0 * half_ref[...]


def body(
    cell_pos,
    cell_drag,
    cell_near,
    analysis,
    stiffness,
    synthesis,
    wall_pos,
    wall_normal,
    wall_weight,
    density,
    patch_near,
    cell_to_patch,
):
    rows, cols, _, points = cell_pos.shape
    size_x, size_y = lax.axis_size("cx"), lax.axis_size("cy")
    near = cell_near.shape[2]
    listed = patch_near.shape[1]
    patches, _, wpoints = wall_pos.shape
    shape = Shape(rows, cols, points, size_x, size_y, near)
    sub, cell = shape.sub, shape.cell
    raw = cell_pos.reshape(rows, cols, 3, sub, LANES)
    raw = jnp.transpose(raw, (0, 2, 3, 1, 4)).reshape(rows * 3 * sub * cols, LANES)
    wtiles = wpoints // LANES
    spare = -(-shape.slots // 8) * 8
    sources = near * points
    assert cell_to_patch.shape[1] == near and patches % 2 == 0
    coef_rows = -(-3 * COEF // 16) * 16
    dma = pltpu.SemaphoreType.DMA
    vmem = pltpu.VMEM
    in_vmem = pl.BlockSpec(memory_space=pltpu.VMEM)
    in_smem = pl.BlockSpec(memory_space=pltpu.SMEM)
    in_hbm = pl.BlockSpec(memory_space=pltpu.HBM)
    walls = lambda v: jnp.transpose(v, (1, 0, 2))
    speed, top, half = pl.pallas_call(
        functools.partial(mega_kernel, shape, listed),
        out_shape=(
            jax.ShapeDtypeStruct(raw.shape, f32),
            jax.ShapeDtypeStruct((sub, LANES), f32),
            jax.ShapeDtypeStruct((3, patches, wpoints), f32),
        ),
        in_specs=[
            in_smem, in_smem, in_hbm, in_hbm, in_hbm, in_hbm,
            in_hbm, in_hbm, in_hbm, in_hbm, in_smem, in_smem,
        ],
        out_specs=[in_vmem] * 3,
        scratch_shapes=[
            vmem(raw.shape, f32),
            vmem((1, stiffness.shape[0]), f32),
            vmem((3, patches, wpoints), f32),
            vmem((3, patches, wpoints), f32),
            vmem((patches, wpoints), f32),
            vmem((3, patches, wpoints), f32),
            vmem(analysis.shape, bf16),
            vmem(synthesis.shape, bf16),
            vmem((spare, cell, LANES), f32),
            vmem((spare, cell, LANES), f32),
            vmem((rows * cols * cell, LANES), f32),
            vmem((24 * sub, LANES), f32),
            vmem((24 * sub, LANES), f32),
            vmem((24 * sub, LANES), f32),
            vmem((24 * sub, LANES), f32),
            vmem((coef_rows * sub, LANES), f32),
            vmem((coef_rows * sub, LANES), f32),
            vmem((coef_rows * sub, LANES), f32),
            vmem((coef_rows * sub, LANES), f32),
            vmem((24 * sub, LANES), f32),
            vmem((points, near * 48), bf16),
            vmem((coef_rows, sources), bf16),
            vmem((points, near * 48), bf16),
            vmem((coef_rows, sources), bf16),
            vmem((rows * cols, (2 * near - 1) * 48, points), bf16),
            vmem((sources, WIDTH), bf16),
            vmem((sources, WIDTH), bf16),
            vmem((coef_rows * sub, LANES), f32),
            vmem((2, 3, patches, wpoints), f32),
            vmem((2, 3, patches, wpoints), f32),
            vmem((2, 3, patches, wpoints), f32),
            vmem((2, patches, wpoints), f32),
            vmem((48 * patches * wtiles, LANES), f32),
            vmem((48 * patches * wtiles, LANES), f32),
            vmem((16 * patches * wtiles, LANES), f32),
            vmem((48 * patches * wtiles, LANES), f32),
            vmem((24 * patches * wtiles, LANES), f32),
            vmem((3 * patches, wpoints, 192), bf16),
            vmem((3 * patches, 16, wpoints), bf16),
            vmem((patches, 192, 2 * wpoints), bf16),
            vmem((patches, near * 48, near * wpoints), bf16),
            vmem((patches * 16 * wtiles, LANES), f32),
            vmem((patches * coef_rows * wtiles, LANES), f32),
            vmem((sub, LANES), f32),
            vmem((sub, LANES), f32),
            vmem((size_y - 1, sub, LANES), f32),
            vmem((size_x - 1, sub, LANES), f32),
            dma((8,)),
            dma((2 * HALO,)),
            dma((2 * HALO,)),
            dma((2 * shape.ext_rows,)),
            dma((2 * shape.ext_rows,)),
            dma((8,)),
            dma((8,)),
            dma((size_y - 1,)),
            dma((size_y - 1,)),
            dma((size_x - 1,)),
            dma((size_x - 1,)),
        ],
        compiler_params=pltpu.CompilerParams(
            collective_id=0, has_side_effects=True, vmem_limit_bytes=62 * 2**20
        ),
        name="mega",
    )(
        jnp.transpose(cell_near, (0, 2, 1)),
        cell_drag,
        raw,
        analysis,
        stiffness[None, :],
        synthesis,
        walls(wall_pos),
        walls(wall_normal),
        wall_weight,
        walls(density),
        jnp.transpose(patch_near),
        jnp.transpose(cell_to_patch),
    )
    moved, dens = pl.pallas_call(
        update_kernel,
        out_shape=(
            jax.ShapeDtypeStruct(raw.shape, f32),
            jax.ShapeDtypeStruct((3, patches, wpoints), f32),
        ),
        in_specs=[in_vmem] * 4,
        out_specs=[in_vmem] * 2,
        name="update",
    )(raw, speed, top, half)
    moved = jnp.transpose(moved.reshape(rows, 3, sub, cols, LANES), (0, 3, 1, 2, 4))
    return moved.reshape(cell_pos.shape), jnp.transpose(dens, (1, 0, 2))


def solution(mesh):
    placed = (
        P("cx", "cy", None, None),
        P("cx", "cy"),
        P("cx", "cy", None),
        P(),
        P(),
        P(),
        P(("cx", "cy"), None, None),
        P(("cx", "cy"), None, None),
        P(("cx", "cy"), None),
        P(("cx", "cy"), None, None),
        P(("cx", "cy"), None),
        P(("cx", "cy"), None),
    )
    return jax.shard_map(
        body,
        mesh=mesh,
        in_specs=placed,
        out_specs=(P("cx", "cy", None, None), P(("cx", "cy"), None, None)),
        check_vma=False,
    )
```

```python
import functools
import math

import jax
import jax.numpy as jnp
from jax import lax
from jax.experimental import pallas as pl
from jax.experimental.pallas import tpu as pltpu
from jax.sharding import PartitionSpec as P

HALO = 3
LANES = 128
WIDTH = 512

soften = 0.25
stokes_scale = 1.0 / (8.0 * math.pi)
layer_scale = 3.0 / (4.0 * math.pi)

MESH = pl.DeviceIdType.MESH
f32 = jnp.float32
bf16 = jnp.bfloat16


def pieces(value):
    high = value.astype(bf16).astype(f32)
    rest = value - high
    middle = rest.astype(bf16).astype(f32)
    return high, middle, rest - middle


def strided(ref, start, count, stride):
    return ref[pl.ds(start, count, stride=stride), :]


def put_wide(ref, first, value):
    tiles = value.shape[1] // LANES
    height = ref.shape[0] // tiles
    for k in range(tiles):
        at = k * height + first
        ref[at : at + value.shape[0], :] = value[:, k * LANES : (k + 1) * LANES]


def get_tile(ref, tiles, tile, start, count, stride):
    height = ref.shape[0] // tiles
    return ref[pl.ds(tile * height + start, count, stride=stride), :]


def get_wide(ref, tiles, start, count, stride):
    return jnp.concatenate([get_tile(ref, tiles, k, start, count, stride) for k in range(tiles)], axis=1)


class Shape:
    def __init__(self, rows, cols, points, size_x, size_y, near):
        self.rows, self.cols, self.points = rows, cols, points
        self.size_x, self.size_y, self.near = size_x, size_y, near
        self.ext_rows = rows + 2 * HALO
        self.sub = points // LANES
        self.cell = 3 * self.sub
        self.left = self.ext_rows * cols
        self.right = self.left + self.ext_rows * HALO
        self.slots = self.right + self.ext_rows * HALO


def cell_slot(shape, gid, me_x, me_y):
    all_rows, all_cols = shape.rows * shape.size_x, shape.cols * shape.size_y
    grid_row = lax.div(gid, jnp.int32(all_cols))
    grid_col = gid - grid_row * all_cols
    row = grid_row - me_x * shape.rows
    row = jnp.where(row < 0, row + all_rows, row)
    row = jnp.where(row >= shape.rows + HALO, row - all_rows + shape.ext_rows, row)
    col = grid_col - me_y * shape.cols + HALO
    col = jnp.where(col < 0, col + all_cols, col)
    col = jnp.where(col >= all_cols, col - all_cols, col)
    middle = row * shape.cols + col - HALO
    left = shape.left + row * HALO + col
    right = shape.right + row * HALO + col - HALO - shape.cols
    slot = jnp.where(col < HALO, left, jnp.where(col >= HALO + shape.cols, right, middle))
    return jnp.clip(slot, 0, shape.slots - 1)


def cell_points(ref, slot, shape):
    block = ref[slot]
    return [block[i * shape.sub : (i + 1) * shape.sub] for i in range(3)]


def put_rows(ref, sub, first, values):
    for i, value in enumerate(values):
        ref[(first + i) * sub : (first + i + 1) * sub, :] = value


def prepare_sources(sources, side_ref, coef_ref, gs, gc, shape, apart):
    sub, points = shape.sub, shape.points
    for n, (y, f) in enumerate(sources):
        square = y[0] * y[0] + y[1] * y[1] + y[2] * y[2]
        split = [pieces(v) for v in (-2.0 * y[0], -2.0 * y[1], -2.0 * y[2], square + soften)]
        for p in range(3):
            put_rows(gs[n], sub, 8 * p, [split[0][p], split[1][p], split[2][p]])
            put_rows(gs[n], sub, 8 * p + 4, [split[3][p]])
        along = y[0] * f[0] + y[1] * f[1] + y[2] * f[2]
        line = [f[0], f[1], f[2], along]
        values = list(line)
        for i in range(3):
            values += [y[i] * v for v in line]
        values += [square * v for v in f]
        for r, value in enumerate(values):
            for p, piece in enumerate(pieces(value)):
                put_rows(gc[n], sub, p * COEF + r, [piece])
    for k in range(sub):
        groups = []
        for n in range(len(sources)):
            h, m, l = [strided(gs[n], p * 8 * sub + k, 8, sub) for p in range(3)]
            groups += [h, m, h, l, h, m]
            rows = strided(gc[n], k, coef_ref.shape[0], sub)
            at = n * points + k * LANES
            coef_ref[:, at : at + LANES] = rows.astype(bf16)
            if apart:
                at = n * points + k * LANES
                side_ref[at : at + LANES, :] = jnp.concatenate(groups, axis=0).T.astype(bf16)
                groups = []
        if not apart:
            block = jnp.concatenate(groups, axis=0).T.astype(bf16)
            side_ref[k * LANES : (k + 1) * LANES, :] = block


COEF = 19


def finish(x, total):
    line = x[0] * total(0) + x[1] * total(1) + x[2] * total(2) - total(3)
    square = x[0] * x[0] + x[1] * x[1] + x[2] * x[2] + 2.0 * soften
    low = [total(i) for i in range(3)]
    near = [[total(4 + 4 * j + i) for i in range(4)] for j in range(3)]
    far = [total(16 + i) for i in range(3)]
    out = []
    for i in range(3):
        cross = x[0] * near[0][i] + x[1] * near[1][i] + x[2] * near[2][i]
        turned = x[0] * near[i][0] + x[1] * near[i][1] + x[2] * near[i][2] - near[i][3]
        direct = square * low[i] + far[i] - 2.0 * cross
        out.append(stokes_scale * (direct + x[i] * line - turned))
    return out


def mega_kernel(
    shape,
    listed,
    near_ref,
    drag_ref,
    pos_hbm,
    analysis_hbm,
    stiffness_hbm,
    synthesis_hbm,
    wpos_hbm,
    wnormal_hbm,
    wweight_hbm,
    wdensity_hbm,
    pnear_ref,
    cpatch_ref,
    speed_hbm,
    top_ref,
    half_ref,
    speed_ref,
    pos_ref,
    stiffness_ref,
    wpos_ref,
    wnormal_ref,
    wweight_ref,
    wdensity_ref,
    analysis_ref,
    synthesis_ref,
    e_ref,
    f_ref,
    v_ref,
    gs_a,
    gs_b,
    gs_c,
    gs_d,
    gc_a,
    gc_b,
    gc_c,
    gc_d,
    gt_ref,
    side_ref,
    cside_ref,
    coef_ref,
    side_b,
    coef_b,
    feats_ref,
    cube_a,
    cube_b,
    h_ref,
    hp_ref,
    hn_ref,
    hd_ref,
    hw_ref,
    gd_ref,
    gq_ref,
    gm_ref,
    gf_ref,
    gw_ref,
    lside_ref,
    lmom_ref,
    lfeat_ref,
    wfeat_ref,
    lacc_ref,
    wacc_ref,
    mine_ref,
    row_ref,
    from_y,
    from_x,
    local,
    xsend,
    xrecv,
    ysend,
    yrecv,
    wsend,
    wrecv,
    tsend_y,
    trecv_y,
    tsend_x,
    trecv_x,
):
    me_x, me_y = lax.axis_index("cx"), lax.axis_index("cy")
    e_cells, f_cells = e_ref, f_ref
    e_ref = e_cells.reshape(e_cells.shape[0] * e_cells.shape[1], LANES)
    f_ref = f_cells.reshape(f_cells.shape[0] * f_cells.shape[1], LANES)
    gs, gc, cubes = (gs_a, gs_b), (gc_a, gc_b), (cube_a, cube_b)
    size_x, size_y = shape.size_x, shape.size_y
    rows, cols, sub, cell = shape.rows, shape.cols, shape.sub, shape.cell
    patches, wpoints = wpos_hbm.shape[1], wpos_hbm.shape[2]
    wtiles = wpoints // LANES

    weights = [
        pltpu.make_async_copy(analysis_hbm, analysis_ref, local.at[0]),
        pltpu.make_async_copy(synthesis_hbm, synthesis_ref, local.at[1]),
        pltpu.make_async_copy(stiffness_hbm, stiffness_ref, local.at[2]),
    ]
    pairs = (
        (pos_hbm, pos_ref), (wpos_hbm, wpos_ref), (wnormal_hbm, wnormal_ref),
        (wweight_hbm, wweight_ref), (wdensity_hbm, wdensity_ref),
    )
    inputs = [pltpu.make_async_copy(src, dst, local.at[3 + k]) for k, (src, dst) in enumerate(pairs)]
    for copy in inputs + weights:
        copy.start()

    def around(step_x, step_y):
        return (lax.rem(me_x + step_x + size_x, size_x), lax.rem(me_y + step_y + size_y, size_y))

    def along_walls(step):
        other = lax.rem(me_x * size_y + me_y + step + size_x * size_y, size_x * size_y)
        there = lax.div(other, jnp.int32(size_y))
        return (there, other - there * size_y)

    peers_y = [around(0, d) for d in range(1, size_y)]
    peers_x = [around(d, 0) for d in range(1, size_x)]
    after, before = along_walls(1), along_walls(-1)
    greeted = peers_y + peers_x + [after, before]
    barrier = pltpu.get_barrier_semaphore()
    for device in greeted:
        pl.semaphore_signal(barrier, inc=1, device_id=device, device_id_type=MESH)

    e_ref[shape.slots * cell :, :] = jnp.zeros_like(e_ref[shape.slots * cell :, :])
    for ref in (*gs, gs_c, gs_d, *gc, gc_c, gc_d, gt_ref, gd_ref, gq_ref, gm_ref, gf_ref, gw_ref):
        ref[...] = jnp.zeros_like(ref)
    one = jnp.ones((sub, LANES), f32)
    for ref in (*gs, gs_c, gs_d):
        ref[3 * sub : 4 * sub, :] = one
    gt_ref[4 * sub : 5 * sub, :] = one
    for copy in inputs:
        copy.wait()
    for r in range(rows):
        for c in range(cols):
            for i in range(3):
                at = ((r * cols + c) * 3 + i) * sub
                e_ref[at : at + sub, :] = strided(pos_ref, (r * 3 + i) * sub * cols + c, sub, cols)

    pl.semaphore_wait(barrier, len(greeted))

    def remote(src, dst, send, recv, device):
        return pltpu.make_async_remote_copy(
            src_ref=src,
            dst_ref=dst,
            send_sem=send,
            recv_sem=recv,
            device_id=device,
            device_id_type=MESH,
        )

    def cells(slot, count):
        return e_cells.at[slot : slot + count]

    xs = []
    for j in range(HALO):
        k = 2 * j
        up = remote(
            cells((rows - HALO + j) * cols, cols),
            cells((rows + HALO + j) * cols, cols),
            xsend.at[k], xrecv.at[k], around(1, 0),
        )
        down = remote(
            cells(j * cols, cols), cells((rows + j) * cols, cols),
            xsend.at[k + 1], xrecv.at[k + 1], around(-1, 0),
        )
        xs += [(up, rows + HALO + j), (down, rows + j)]

    def sideways(row):
        right = remote(
            cells(row * cols + cols - HALO, HALO), cells(shape.left + row * HALO, HALO),
            ysend.at[2 * row], yrecv.at[2 * row], around(0, 1),
        )
        left = remote(
            cells(row * cols, HALO), cells(shape.right + row * HALO, HALO),
            ysend.at[2 * row + 1], yrecv.at[2 * row + 1], around(0, -1),
        )
        return [right, left]

    ws = []
    sources = ((wpos_ref, hp_ref), (wnormal_ref, hn_ref), (wdensity_ref, hd_ref), (wweight_ref, hw_ref))
    for b, device in enumerate((after, before)):
        for src, dst in sources:
            k = len(ws)
            ws.append(remote(src, dst.at[b], wsend.at[k], wrecv.at[k], device))

    for copy in ws:
        copy.start()
    for copy, _ in xs:
        copy.start()
    ys = []
    for row in range(rows):
        for copy in sideways(row):
            copy.start()
            ys.append(copy)

    def target(i, _):
        x = cell_points(e_cells, i, shape)
        square = x[0] * x[0] + x[1] * x[1] + x[2] * x[2]
        split = [pieces(v) for v in (x[0], x[1], x[2], square)]
        for p in range(3):
            put_rows(gt_ref, sub, 8 * p, [s[p] for s in split])
        tiles = []
        for k in range(sub):
            h, m, l = [strided(gt_ref, p * 8 * sub + k, 8, sub) for p in range(3)]
            tiles.append(jnp.concatenate([h, h, m, h, l, m], axis=0).astype(bf16))
        feats_ref[i] = jnp.concatenate(tiles, axis=1)
        return 0

    lax.fori_loop(0, rows * cols, target, 0)

    x = [wpos_ref[i] for i in range(3)]
    lone = jnp.ones((patches, wpoints), f32)
    squares = [x[i] * x[i] for i in range(3)]
    mono = x + [lone] + squares + [x[0] * x[1], x[0] * x[2], x[1] * x[2]]
    square = squares[0] + squares[1] + squares[2]
    for r, value in enumerate(mono):
        for p, piece in enumerate(pieces(value)):
            put_wide(gf_ref, (16 * p + r) * patches, piece)
    for r, value in enumerate(x + [square, lone]):
        for p, piece in enumerate(pieces(value)):
            put_wide(gw_ref, (8 * p + r) * patches, piece)
    for q in range(patches):
        h, m, l = [get_wide(gf_ref, wtiles, p * 16 * patches + q, 16, patches) for p in range(3)]
        wide = jnp.concatenate([h, h, m, h, l, m], axis=0).astype(bf16)
        blank = jnp.zeros_like(wide)
        for k in range(2):
            rows2 = [wide if j == k else blank for j in range(2)]
            lfeat_ref[q, :, k * wpoints : (k + 1) * wpoints] = jnp.concatenate(rows2, axis=0)
        h, m, l = [get_wide(gw_ref, wtiles, p * 8 * patches + q, 8, patches) for p in range(3)]
        wide = jnp.concatenate([h, h, m, h, l, m], axis=0).astype(bf16)
        blank = jnp.zeros_like(wide)
        for k in range(shape.near):
            rows2 = [wide if j == k else blank for j in range(shape.near)]
            wfeat_ref[q, :, k * wpoints : (k + 1) * wpoints] = jnp.concatenate(rows2, axis=0)

    def wall_sources(b, y, n, v, w):
        w = -layer_scale * w
        v = [w * value for value in v]
        zero = jnp.zeros_like(w)
        ones = jnp.ones_like(w)
        square = y[0] * y[0] + y[1] * y[1] + y[2] * y[2] + soften
        dist = [-2.0 * y[0], -2.0 * y[1], -2.0 * y[2], square, ones, ones, ones]
        a = y[0] * v[0] + y[1] * v[1] + y[2] * v[2]
        c = y[0] * n[0] + y[1] * n[1] + y[2] * n[2]
        quad = [-(v[i] * c + n[i] * a) for i in range(3)] + [a * c]
        quad += [v[i] * n[i] for i in range(3)]
        quad += [v[i] * n[j] + v[j] * n[i] for i, j in ((0, 1), (0, 2), (1, 2))]
        for values, ref in ((dist, gd_ref), (quad, gq_ref)):
            for r, value in enumerate(values):
                for p, piece in enumerate(pieces(value)):
                    put_wide(ref, (16 * p + r) * patches, piece)
        for r, value in enumerate(y + [ones]):
            for p, piece in enumerate(pieces(value)):
                if p == 0 or r < 3:
                    put_wide(gm_ref, (4 * p + r) * patches, piece)

        def one_patch(q, _):
            slot = b * patches + q
            for k in range(wtiles):
                groups = []
                for ref in (gd_ref, gq_ref):
                    h, m, l = [
                        get_tile(ref, wtiles, k, p * 16 * patches + q, 16, patches) for p in range(3)
                    ]
                    groups += [h, m, h, l, h, m]
                block = jnp.concatenate(groups, axis=0).T.astype(bf16)
                lside_ref[slot, k * LANES : (k + 1) * LANES, :] = block
            rows16 = get_wide(gm_ref, wtiles, q, 16, patches)
            lmom_ref[slot] = rows16.astype(bf16)
            return 0

        lax.fori_loop(0, patches, one_patch, 0, unroll=2)

    wall_sources(
        1, x, [wnormal_ref[i] for i in range(3)], [wdensity_ref[i] for i in range(3)], wweight_ref[...]
    )

    for copy in weights:
        copy.wait()

    def membrane(first, count):
        tiles = [strided(e_ref, first * sub + k, count, sub) for k in range(sub)]
        value = jnp.concatenate(tiles, axis=1)
        centred = (value - jnp.mean(value, axis=1, keepdims=True)).astype(bf16)
        coeff = jnp.dot(centred, analysis_ref[...], preferred_element_type=f32)
        scaled = (coeff * stiffness_ref[...]).astype(bf16)
        force = -jnp.dot(scaled, synthesis_ref[...], preferred_element_type=f32)
        for k in range(sub):
            f_ref[pl.ds(first * sub + k, count, stride=sub), :] = force[:, k * LANES : (k + 1) * LANES]

    membrane(0, 3 * rows * cols)

    def pass_on(pairs):
        for copy, row in pairs:
            copy.wait_recv()
            for onward in sideways(row):
                onward.start()
                ys.append(onward)

    all_patches = patches * size_x * size_y
    block_start = (me_x * size_y + me_y) * patches

    def put_patch(ref, t, value):
        height = ref.shape[0] // wtiles
        for k in range(wtiles):
            at = pl.multiple_of(k * height + t * value.shape[0], 8)
            ref[pl.ds(at, value.shape[0]), :] = value[:, k * LANES : (k + 1) * LANES]

    def layer_slot(t, n):
        if n == 0:
            return t + patches
        slot = pnear_ref[n - 1, t] - block_start + patches
        slot = jnp.where(slot < 0, slot + all_patches, slot)
        slot = jnp.where(slot >= all_patches, slot - all_patches, slot)
        return jnp.clip(slot, 0, 3 * patches - 1)

    def layer_pair(j, _):
        slots = [[layer_slot(2 * j + u, n) for n in range(listed + 1)] for u in range(2)]
        scalars = []
        for u in range(2):
            side = jnp.concatenate([lside_ref[slot] for slot in slots[u]], axis=0)
            both = jnp.dot(side, lfeat_ref[2 * j + u], preferred_element_type=f32)
            root = lax.rsqrt(both[:, :wpoints])
            square = root * root
            scalars.append((both[:, wpoints:] * (square * square * root)).astype(bf16))
        moment = jnp.concatenate(
            [jnp.concatenate([lmom_ref[slot] for slot in slots[u]], axis=1) for u in range(2)], axis=0
        )
        total = jnp.dot(moment, jnp.concatenate(scalars, axis=1), preferred_element_type=f32)
        for u in range(2):
            put_patch(lacc_ref, 2 * j + u, total[16 * u : 16 * u + 16, u * wpoints : (u + 1) * wpoints])
        return 0

    pass_on(xs[:1])
    for copy in ws:
        copy.wait_recv()
    for b in range(1):
        wall_sources(
            2 * b,
            [hp_ref[b, i] for i in range(3)],
            [hn_ref[b, i] for i in range(3)],
            [hd_ref[b, i] for i in range(3)],
            hw_ref[b],
        )

    pass_on(xs[1:2])
    for b in range(1, 2):
        wall_sources(
            2 * b,
            [hp_ref[b, i] for i in range(3)],
            [hn_ref[b, i] for i in range(3)],
            [hd_ref[b, i] for i in range(3)],
            hw_ref[b],
        )

    pass_on(xs[2:4])
    lax.fori_loop(0, 1, layer_pair, 0)
    pass_on(xs[4:5])
    lax.fori_loop(1, 2, layer_pair, 0)
    pass_on(xs[5:])
    lax.fori_loop(2, patches // 2, layer_pair, 0)

    for copy in ys:
        copy.wait_recv()
    membrane(3 * rows * cols, -(-3 * (shape.slots - rows * cols) // 8) * 8)

    def prepare(gids, side_ref, coef_ref, gs, gc, apart=False):
        slots = [cell_slot(shape, gid, me_x, me_y) for gid in gids]
        sources = [(cell_points(e_cells, k, shape), cell_points(f_cells, k, shape)) for k in slots]
        prepare_sources(sources, side_ref, coef_ref, gs, gc, shape, apart)

    def cell_prepare(i):
        r = lax.div(i, jnp.int32(cols))
        c = i - r * cols
        gids = [near_ref[r, n, c] for n in range(shape.near)]
        prepare(gids, cside_ref, coef_ref, gs, gc, True)

    chunks = shape.points // WIDTH
    half = shape.near * 48
    parts = []
    for n in range(shape.near):
        parts.append((None, n, slice(n * shape.points, (n + 1) * shape.points)))

    def weigh(part, cube_ref):
        return jnp.dot(coef_ref[:, part], cube_ref[part, :], preferred_element_type=f32)

    def keep(t, acc):
        for k in range(WIDTH // LANES):
            tile = t * (WIDTH // LANES) + k
            h_ref[pl.ds(tile, acc.shape[0], stride=sub), :] = acc[:, k * LANES : (k + 1) * LANES]

    def cell_sums(i):
        for t in range(chunks):
            acc = None
            for near_rows, n, part in parts:
                feat = feats_ref[i, :, t * WIDTH : (t + 1) * WIDTH]
                root = lax.rsqrt(jnp.dot(cside_ref[part, :], feat, preferred_element_type=f32))
                cubes[t % 2][part, :] = (root * root * root).astype(bf16)
                if t > 0:
                    more = weigh(part, cubes[(t - 1) % 2])
                    acc = more if acc is None else acc + more
            if t > 0:
                keep(t - 1, acc)
        acc = None
        for _, _, part in parts:
            more = weigh(part, cubes[(chunks - 1) % 2])
            acc = more if acc is None else acc + more
        keep(chunks - 1, acc)

    def cell_finish(i, best):
        r = lax.div(i, jnp.int32(cols))
        c = i - r * cols
        x = cell_points(e_cells, i, shape)

        def total(row):
            a, b, d = [h_ref[(p * COEF + row) * sub : (p * COEF + row + 1) * sub, :] for p in range(3)]
            return a + (b + d)

        parts = finish(x, total)
        own = cell_points(f_cells, i, shape)
        drag = drag_ref[r, c]
        squared = jnp.zeros_like(best)
        values = []
        for k in range(3):
            value = drag * own[k] + parts[k]
            values.append(value)
            squared = squared + value * value
        v_ref[pl.ds(pl.multiple_of(i * cell, 8), cell), :] = jnp.concatenate(values, axis=0)
        return jnp.maximum(best, squared)

    def cell_step(i, best):
        cell_sums(i)
        cell_prepare(jnp.minimum(i + 1, rows * cols - 1))
        return cell_finish(i, best)

    cell_prepare(jnp.int32(0))
    best = lax.fori_loop(0, rows * cols, cell_step, jnp.zeros((sub, LANES), f32))
    mine_ref[...] = best

    sets = ((side_ref, coef_ref, gs, gc), (side_b, coef_b, (gs_c, gs_d), (gc_c, gc_d)))

    def wall_prepare(j):
        for u in range(2):
            gids = [cpatch_ref[n, 2 * j + u] for n in range(shape.near)]
            prepare(gids, *sets[u])

    def wall_pair(j, _):
        accs = [None, None]
        for at in range(0, shape.points, WIDTH):
            cubes2 = []
            for u in range(2):
                square = jnp.dot(
                    sets[u][0][at : at + WIDTH, :], wfeat_ref[2 * j + u], preferred_element_type=f32
                )
                root = lax.rsqrt(square)
                cubes2.append((root * root * root).astype(bf16))
            for u in range(2):
                coef = sets[u][1]
                both = jnp.concatenate(
                    [coef[:, n * shape.points + at : n * shape.points + at + WIDTH] for n in range(shape.near)],
                    axis=0,
                )
                more = jnp.dot(both, cubes2[u], preferred_element_type=f32)
                accs[u] = more if accs[u] is None else accs[u] + more
        count = coef_ref.shape[0]
        for u in range(2):
            blocks = [
                accs[u][n * count : (n + 1) * count, n * wpoints : (n + 1) * wpoints]
                for n in range(shape.near)
            ]
            put_patch(wacc_ref, 2 * j + u, functools.reduce(jnp.add, blocks))
        wall_prepare(jnp.minimum(j + 1, patches // 2 - 1))
        return 0

    for r in range(rows):
        for c in range(cols):
            for i in range(3):
                at = ((r * cols + c) * 3 + i) * sub
                speed_ref[pl.ds((r * 3 + i) * sub * cols + c, sub, stride=cols), :] = v_ref[at : at + sub, :]
    wall_prepare(jnp.int32(0))
    copies = []
    for d, device in enumerate(peers_y):
        copies.append(remote(mine_ref, from_y.at[d], tsend_y.at[d], trecv_y.at[d], device))
        copies[-1].start()
    lax.fori_loop(0, 1, wall_pair, 0)
    speeds = pltpu.make_async_copy(speed_ref, speed_hbm, local.at[8])
    speeds.start()
    best = mine_ref[...]
    for d, copy in enumerate(copies):
        copy.wait_recv()
        best = jnp.maximum(best, from_y[d])
    row_ref[...] = best
    moment = [get_wide(lacc_ref, wtiles, r, patches, 16) for r in range(11)]
    moment = [moment[i] + (moment[4 + i] + moment[8 + i]) for i in range(3)] + [moment[3]]
    for i in range(3):
        half_ref[i] = x[i] * moment[3] - moment[i]
    for d, device in enumerate(peers_x):
        copies.append(remote(row_ref, from_x.at[d], tsend_x.at[d], trecv_x.at[d], device))
        copies[-1].start()
    lax.fori_loop(1, patches // 2, wall_pair, 0)

    def wall_total(row):
        a, b, d = [
            get_wide(wacc_ref, wtiles, p * COEF + row, patches, coef_ref.shape[0]) for p in range(3)
        ]
        return a + (b + d)

    flow = finish(x, wall_total)
    for i in range(3):
        half_ref[i] = half_ref[i] + flow[i]

    best = row_ref[...]
    for d, copy in enumerate(copies[size_y - 1 :]):
        copy.wait_recv()
        best = jnp.maximum(best, from_x[d])
    top_ref[...] = best
    speeds.wait()
    for copy, _ in xs:
        copy.wait_send()
    for copy in ws + ys + copies:
        copy.wait_send()


def update_kernel(pos_ref, speed_ref, top_ref, half_ref, moved_ref, dens_ref):
    top = jnp.sqrt(jnp.max(top_ref[...], keepdims=True))
    step = 1.0 / (top + 1e-06)
    moved_ref[...] = pos_ref[...] + step * speed_ref[...]
    dens_ref[...] = 2.0 * half_ref[...]


def body(
    cell_pos,
    cell_drag,
    cell_near,
    analysis,
    stiffness,
    synthesis,
    wall_pos,
    wall_normal,
    wall_weight,
    density,
    patch_near,
    cell_to_patch,
):
    rows, cols, _, points = cell_pos.shape
    size_x, size_y = lax.axis_size("cx"), lax.axis_size("cy")
    near = cell_near.shape[2]
    listed = patch_near.shape[1]
    patches, _, wpoints = wall_pos.shape
    shape = Shape(rows, cols, points, size_x, size_y, near)
    sub, cell = shape.sub, shape.cell
    raw = cell_pos.reshape(rows, cols, 3, sub, LANES)
    raw = jnp.transpose(raw, (0, 2, 3, 1, 4)).reshape(rows * 3 * sub * cols, LANES)
    wtiles = wpoints // LANES
    spare = -(-shape.slots // 8) * 8
    sources = near * points
    assert cell_to_patch.shape[1] == near and patches % 2 == 0
    coef_rows = -(-3 * COEF // 16) * 16
    dma = pltpu.SemaphoreType.DMA
    vmem = pltpu.VMEM
    in_vmem = pl.BlockSpec(memory_space=pltpu.VMEM)
    in_smem = pl.BlockSpec(memory_space=pltpu.SMEM)
    in_hbm = pl.BlockSpec(memory_space=pltpu.HBM)
    walls = lambda v: jnp.transpose(v, (1, 0, 2))
    speed, top, half = pl.pallas_call(
        functools.partial(mega_kernel, shape, listed),
        out_shape=(
            jax.ShapeDtypeStruct(raw.shape, f32),
            jax.ShapeDtypeStruct((sub, LANES), f32),
            jax.ShapeDtypeStruct((3, patches, wpoints), f32),
        ),
        in_specs=[
            in_smem, in_smem, in_hbm, in_hbm, in_hbm, in_hbm,
            in_hbm, in_hbm, in_hbm, in_hbm, in_smem, in_smem,
        ],
        out_specs=[in_hbm, in_vmem, in_vmem],
        scratch_shapes=[
            vmem(raw.shape, f32),
            vmem(raw.shape, f32),
            vmem((1, stiffness.shape[0]), f32),
            vmem((3, patches, wpoints), f32),
            vmem((3, patches, wpoints), f32),
            vmem((patches, wpoints), f32),
            vmem((3, patches, wpoints), f32),
            vmem(analysis.shape, bf16),
            vmem(synthesis.shape, bf16),
            vmem((spare, cell, LANES), f32),
            vmem((spare, cell, LANES), f32),
            vmem((rows * cols * cell, LANES), f32),
            vmem((24 * sub, LANES), f32),
            vmem((24 * sub, LANES), f32),
            vmem((24 * sub, LANES), f32),
            vmem((24 * sub, LANES), f32),
            vmem((coef_rows * sub, LANES), f32),
            vmem((coef_rows * sub, LANES), f32),
            vmem((coef_rows * sub, LANES), f32),
            vmem((coef_rows * sub, LANES), f32),
            vmem((24 * sub, LANES), f32),
            vmem((points, near * 48), bf16),
            vmem((sources, 48), bf16),
            vmem((coef_rows, sources), bf16),
            vmem((points, near * 48), bf16),
            vmem((coef_rows, sources), bf16),
            vmem((rows * cols, 48, points), bf16),
            vmem((sources, WIDTH), bf16),
            vmem((sources, WIDTH), bf16),
            vmem((coef_rows * sub, LANES), f32),
            vmem((2, 3, patches, wpoints), f32),
            vmem((2, 3, patches, wpoints), f32),
            vmem((2, 3, patches, wpoints), f32),
            vmem((2, patches, wpoints), f32),
            vmem((48 * patches * wtiles, LANES), f32),
            vmem((48 * patches * wtiles, LANES), f32),
            vmem((16 * patches * wtiles, LANES), f32),
            vmem((48 * patches * wtiles, LANES), f32),
            vmem((24 * patches * wtiles, LANES), f32),
            vmem((3 * patches, wpoints, 192), bf16),
            vmem((3 * patches, 16, wpoints), bf16),
            vmem((patches, 192, 2 * wpoints), bf16),
            vmem((patches, near * 48, near * wpoints), bf16),
            vmem((patches * 16 * wtiles, LANES), f32),
            vmem((patches * coef_rows * wtiles, LANES), f32),
            vmem((sub, LANES), f32),
            vmem((sub, LANES), f32),
            vmem((size_y - 1, sub, LANES), f32),
            vmem((size_x - 1, sub, LANES), f32),
            dma((9,)),
            dma((2 * HALO,)),
            dma((2 * HALO,)),
            dma((2 * shape.ext_rows,)),
            dma((2 * shape.ext_rows,)),
            dma((8,)),
            dma((8,)),
            dma((size_y - 1,)),
            dma((size_y - 1,)),
            dma((size_x - 1,)),
            dma((size_x - 1,)),
        ],
        compiler_params=pltpu.CompilerParams(
            collective_id=0, has_side_effects=True, vmem_limit_bytes=62 * 2**20
        ),
        name="mega",
    )(
        jnp.transpose(cell_near, (0, 2, 1)),
        cell_drag,
        raw,
        analysis,
        stiffness[None, :],
        synthesis,
        walls(wall_pos),
        walls(wall_normal),
        wall_weight,
        walls(density),
        jnp.transpose(patch_near),
        jnp.transpose(cell_to_patch),
    )
    moved, dens = pl.pallas_call(
        update_kernel,
        out_shape=(
            jax.ShapeDtypeStruct(raw.shape, f32),
            jax.ShapeDtypeStruct((3, patches, wpoints), f32),
        ),
        in_specs=[in_vmem] * 4,
        out_specs=[in_vmem] * 2,
        name="update",
    )(raw, speed, top, half)
    moved = jnp.transpose(moved.reshape(rows, 3, sub, cols, LANES), (0, 3, 1, 2, 4))
    return moved.reshape(cell_pos.shape), jnp.transpose(dens, (1, 0, 2))


def solution(mesh):
    placed = (
        P("cx", "cy", None, None),
        P("cx", "cy"),
        P("cx", "cy", None),
        P(),
        P(),
        P(),
        P(("cx", "cy"), None, None),
        P(("cx", "cy"), None, None),
        P(("cx", "cy"), None),
        P(("cx", "cy"), None, None),
        P(("cx", "cy"), None),
        P(("cx", "cy"), None),
    )
    return jax.shard_map(
        body,
        mesh=mesh,
        in_specs=placed,
        out_specs=(P("cx", "cy", None, None), P(("cx", "cy"), None, None)),
        check_vma=False,
    )
```

```python
import functools
import math

import jax
import jax.numpy as jnp
from jax import lax
from jax.experimental import pallas as pl
from jax.experimental.pallas import tpu as pltpu
from jax.sharding import PartitionSpec as P

HALO = 3
LANES = 128
WIDTH = 512

soften = 0.25
stokes_scale = 1.0 / (8.0 * math.pi)
layer_scale = 3.0 / (4.0 * math.pi)

MESH = pl.DeviceIdType.MESH
f32 = jnp.float32
bf16 = jnp.bfloat16


def pieces(value):
    high = value.astype(bf16).astype(f32)
    rest = value - high
    middle = rest.astype(bf16).astype(f32)
    return high, middle, rest - middle


def strided(ref, start, count, stride):
    return ref[pl.ds(start, count, stride=stride), :]


def put_wide(ref, first, value):
    tiles = value.shape[1] // LANES
    height = ref.shape[0] // tiles
    for k in range(tiles):
        at = k * height + first
        ref[at : at + value.shape[0], :] = value[:, k * LANES : (k + 1) * LANES]


def get_tile(ref, tiles, tile, start, count, stride):
    height = ref.shape[0] // tiles
    return ref[pl.ds(tile * height + start, count, stride=stride), :]


def get_wide(ref, tiles, start, count, stride):
    return jnp.concatenate([get_tile(ref, tiles, k, start, count, stride) for k in range(tiles)], axis=1)


class Shape:
    def __init__(self, rows, cols, points, size_x, size_y, near):
        self.rows, self.cols, self.points = rows, cols, points
        self.size_x, self.size_y, self.near = size_x, size_y, near
        self.ext_rows = rows + 2 * HALO
        self.sub = points // LANES
        self.cell = 3 * self.sub
        self.left = self.ext_rows * cols
        self.right = self.left + self.ext_rows * HALO
        self.slots = self.right + self.ext_rows * HALO


def cell_slot(shape, gid, me_x, me_y):
    all_rows, all_cols = shape.rows * shape.size_x, shape.cols * shape.size_y
    grid_row = lax.div(gid, jnp.int32(all_cols))
    grid_col = gid - grid_row * all_cols
    row = grid_row - me_x * shape.rows
    row = jnp.where(row < 0, row + all_rows, row)
    row = jnp.where(row >= shape.rows + HALO, row - all_rows + shape.ext_rows, row)
    col = grid_col - me_y * shape.cols + HALO
    col = jnp.where(col < 0, col + all_cols, col)
    col = jnp.where(col >= all_cols, col - all_cols, col)
    middle = row * shape.cols + col - HALO
    left = shape.left + row * HALO + col
    right = shape.right + row * HALO + col - HALO - shape.cols
    slot = jnp.where(col < HALO, left, jnp.where(col >= HALO + shape.cols, right, middle))
    return jnp.clip(slot, 0, shape.slots - 1)


def cell_points(ref, slot, shape):
    block = ref[slot]
    return [block[i * shape.sub : (i + 1) * shape.sub] for i in range(3)]


def put_rows(ref, sub, first, values):
    for i, value in enumerate(values):
        ref[(first + i) * sub : (first + i + 1) * sub, :] = value


def prepare_sources(sources, side_ref, coef_ref, gs, gc, shape, apart):
    sub, points = shape.sub, shape.points
    for n, (y, f) in enumerate(sources):
        square = y[0] * y[0] + y[1] * y[1] + y[2] * y[2]
        split = [pieces(v) for v in (-2.0 * y[0], -2.0 * y[1], -2.0 * y[2], square + soften)]
        for p in range(3):
            put_rows(gs[n], sub, 8 * p, [split[0][p], split[1][p], split[2][p]])
            put_rows(gs[n], sub, 8 * p + 4, [split[3][p]])
        along = y[0] * f[0] + y[1] * f[1] + y[2] * f[2]
        line = [f[0], f[1], f[2], along]
        values = list(line)
        for i in range(3):
            values += [y[i] * v for v in line]
        values += [square * v for v in f]
        for r, value in enumerate(values):
            for p, piece in enumerate(pieces(value)):
                put_rows(gc[n], sub, p * COEF + r, [piece])
    for k in range(sub):
        groups = []
        for n in range(len(sources)):
            h, m, l = [strided(gs[n], p * 8 * sub + k, 8, sub) for p in range(3)]
            groups += [h, m, h, l, h, m]
            rows = strided(gc[n], k, coef_ref.shape[0], sub)
            at = n * points + k * LANES
            coef_ref[:, at : at + LANES] = rows.astype(bf16)
            if apart:
                at = n * points + k * LANES
                side_ref[at : at + LANES, :] = jnp.concatenate(groups, axis=0).T.astype(bf16)
                groups = []
        if not apart:
            block = jnp.concatenate(groups, axis=0).T.astype(bf16)
            side_ref[k * LANES : (k + 1) * LANES, :] = block


COEF = 19


def finish(x, total):
    line = x[0] * total(0) + x[1] * total(1) + x[2] * total(2) - total(3)
    square = x[0] * x[0] + x[1] * x[1] + x[2] * x[2] + 2.0 * soften
    low = [total(i) for i in range(3)]
    near = [[total(4 + 4 * j + i) for i in range(4)] for j in range(3)]
    far = [total(16 + i) for i in range(3)]
    out = []
    for i in range(3):
        cross = x[0] * near[0][i] + x[1] * near[1][i] + x[2] * near[2][i]
        turned = x[0] * near[i][0] + x[1] * near[i][1] + x[2] * near[i][2] - near[i][3]
        direct = square * low[i] + far[i] - 2.0 * cross
        out.append(stokes_scale * (direct + x[i] * line - turned))
    return out


def mega_kernel(
    shape,
    listed,
    near_ref,
    drag_ref,
    pos_hbm,
    analysis_hbm,
    stiffness_hbm,
    synthesis_hbm,
    wpos_hbm,
    wnormal_hbm,
    wweight_hbm,
    wdensity_hbm,
    pnear_ref,
    cpatch_ref,
    speed_hbm,
    top_ref,
    half_ref,
    speed_ref,
    pos_ref,
    stiffness_ref,
    wpos_ref,
    wnormal_ref,
    wweight_ref,
    wdensity_ref,
    analysis_ref,
    synthesis_ref,
    e_ref,
    f_ref,
    v_ref,
    gs_a,
    gs_b,
    gs_c,
    gs_d,
    gc_a,
    gc_b,
    gc_c,
    gc_d,
    gt_ref,
    side_ref,
    cside_ref,
    coef_ref,
    side_b,
    coef_b,
    feats_ref,
    cube_a,
    cube_b,
    h_ref,
    hp_ref,
    hn_ref,
    hd_ref,
    hw_ref,
    gd_ref,
    gq_ref,
    gm_ref,
    gf_ref,
    gw_ref,
    lside_ref,
    lmom_ref,
    lfeat_ref,
    wfeat_ref,
    lacc_ref,
    wacc_ref,
    mine_ref,
    row_ref,
    from_y,
    from_x,
    local,
    xsend,
    xrecv,
    ysend,
    yrecv,
    wsend,
    wrecv,
    tsend_y,
    trecv_y,
    tsend_x,
    trecv_x,
):
    me_x, me_y = lax.axis_index("cx"), lax.axis_index("cy")
    e_cells, f_cells = e_ref, f_ref
    e_ref = e_cells.reshape(e_cells.shape[0] * e_cells.shape[1], LANES)
    f_ref = f_cells.reshape(f_cells.shape[0] * f_cells.shape[1], LANES)
    gs, gc, cubes = (gs_a, gs_b), (gc_a, gc_b), (cube_a, cube_b)
    size_x, size_y = shape.size_x, shape.size_y
    rows, cols, sub, cell = shape.rows, shape.cols, shape.sub, shape.cell
    patches, wpoints = wpos_hbm.shape[1], wpos_hbm.shape[2]
    wtiles = wpoints // LANES

    weights = [
        pltpu.make_async_copy(analysis_hbm, analysis_ref, local.at[0]),
        pltpu.make_async_copy(synthesis_hbm, synthesis_ref, local.at[1]),
        pltpu.make_async_copy(stiffness_hbm, stiffness_ref, local.at[2]),
    ]
    pairs = (
        (pos_hbm, pos_ref), (wpos_hbm, wpos_ref), (wnormal_hbm, wnormal_ref),
        (wweight_hbm, wweight_ref), (wdensity_hbm, wdensity_ref),
    )
    inputs = [pltpu.make_async_copy(src, dst, local.at[3 + k]) for k, (src, dst) in enumerate(pairs)]
    for copy in inputs + weights:
        copy.start()

    def around(step_x, step_y):
        return (lax.rem(me_x + step_x + size_x, size_x), lax.rem(me_y + step_y + size_y, size_y))

    def along_walls(step):
        other = lax.rem(me_x * size_y + me_y + step + size_x * size_y, size_x * size_y)
        there = lax.div(other, jnp.int32(size_y))
        return (there, other - there * size_y)

    peers_y = [around(0, d) for d in range(1, size_y)]
    peers_x = [around(d, 0) for d in range(1, size_x)]
    after, before = along_walls(1), along_walls(-1)
    greeted = peers_y + peers_x + [after, before]
    barrier = pltpu.get_barrier_semaphore()
    for device in greeted:
        pl.semaphore_signal(barrier, inc=1, device_id=device, device_id_type=MESH)

    e_ref[shape.slots * cell :, :] = jnp.zeros_like(e_ref[shape.slots * cell :, :])
    for ref in (*gs, gs_c, gs_d, *gc, gc_c, gc_d, gt_ref, gd_ref, gq_ref, gm_ref, gf_ref, gw_ref):
        ref[...] = jnp.zeros_like(ref)
    one = jnp.ones((sub, LANES), f32)
    for ref in (*gs, gs_c, gs_d):
        ref[3 * sub : 4 * sub, :] = one
    gt_ref[4 * sub : 5 * sub, :] = one
    for copy in inputs:
        copy.wait()
    for r in range(rows):
        for c in range(cols):
            for i in range(3):
                at = ((r * cols + c) * 3 + i) * sub
                e_ref[at : at + sub, :] = strided(pos_ref, (r * 3 + i) * sub * cols + c, sub, cols)

    pl.semaphore_wait(barrier, len(greeted))

    def remote(src, dst, send, recv, device):
        return pltpu.make_async_remote_copy(
            src_ref=src,
            dst_ref=dst,
            send_sem=send,
            recv_sem=recv,
            device_id=device,
            device_id_type=MESH,
        )

    def cells(slot, count):
        return e_cells.at[slot : slot + count]

    xs = []
    for j in range(HALO):
        k = 2 * j
        up = remote(
            cells((rows - HALO + j) * cols, cols),
            cells((rows + HALO + j) * cols, cols),
            xsend.at[k], xrecv.at[k], around(1, 0),
        )
        down = remote(
            cells(j * cols, cols), cells((rows + j) * cols, cols),
            xsend.at[k + 1], xrecv.at[k + 1], around(-1, 0),
        )
        xs += [(up, rows + HALO + j), (down, rows + j)]

    def sideways(row):
        right = remote(
            cells(row * cols + cols - HALO, HALO), cells(shape.left + row * HALO, HALO),
            ysend.at[2 * row], yrecv.at[2 * row], around(0, 1),
        )
        left = remote(
            cells(row * cols, HALO), cells(shape.right + row * HALO, HALO),
            ysend.at[2 * row + 1], yrecv.at[2 * row + 1], around(0, -1),
        )
        return [right, left]

    ws = []
    sources = ((wpos_ref, hp_ref), (wnormal_ref, hn_ref), (wdensity_ref, hd_ref), (wweight_ref, hw_ref))
    for b, device in enumerate((after, before)):
        for src, dst in sources:
            k = len(ws)
            ws.append(remote(src, dst.at[b], wsend.at[k], wrecv.at[k], device))

    for copy in ws:
        copy.start()
    for copy, _ in xs:
        copy.start()
    ys = []
    for row in range(rows):
        for copy in sideways(row):
            copy.start()
            ys.append(copy)

    def target(i, _):
        x = cell_points(e_cells, i, shape)
        square = x[0] * x[0] + x[1] * x[1] + x[2] * x[2]
        split = [pieces(v) for v in (x[0], x[1], x[2], square)]
        for p in range(3):
            put_rows(gt_ref, sub, 8 * p, [s[p] for s in split])
        tiles = []
        for k in range(sub):
            h, m, l = [strided(gt_ref, p * 8 * sub + k, 8, sub) for p in range(3)]
            tiles.append(jnp.concatenate([h, h, m, h, l, m], axis=0).astype(bf16))
        feats_ref[i] = jnp.concatenate(tiles, axis=1)
        return 0

    lax.fori_loop(0, rows * cols, target, 0)

    x = [wpos_ref[i] for i in range(3)]
    lone = jnp.ones((patches, wpoints), f32)
    squares = [x[i] * x[i] for i in range(3)]
    mono = x + [lone] + squares + [x[0] * x[1], x[0] * x[2], x[1] * x[2]]
    square = squares[0] + squares[1] + squares[2]
    for r, value in enumerate(mono):
        for p, piece in enumerate(pieces(value)):
            put_wide(gf_ref, (16 * p + r) * patches, piece)
    for r, value in enumerate(x + [square, lone]):
        for p, piece in enumerate(pieces(value)):
            put_wide(gw_ref, (8 * p + r) * patches, piece)
    for q in range(patches):
        h, m, l = [get_wide(gf_ref, wtiles, p * 16 * patches + q, 16, patches) for p in range(3)]
        wide = jnp.concatenate([h, h, m, h, l, m], axis=0).astype(bf16)
        blank = jnp.zeros_like(wide)
        for k in range(2):
            rows2 = [wide if j == k else blank for j in range(2)]
            lfeat_ref[q, :, k * wpoints : (k + 1) * wpoints] = jnp.concatenate(rows2, axis=0)
        h, m, l = [get_wide(gw_ref, wtiles, p * 8 * patches + q, 8, patches) for p in range(3)]
        wide = jnp.concatenate([h, h, m, h, l, m], axis=0).astype(bf16)
        blank = jnp.zeros_like(wide)
        for k in range(shape.near):
            rows2 = [wide if j == k else blank for j in range(shape.near)]
            wfeat_ref[q, :, k * wpoints : (k + 1) * wpoints] = jnp.concatenate(rows2, axis=0)

    def wall_sources(b, y, n, v, w):
        w = -layer_scale * w
        v = [w * value for value in v]
        zero = jnp.zeros_like(w)
        ones = jnp.ones_like(w)
        square = y[0] * y[0] + y[1] * y[1] + y[2] * y[2] + soften
        dist = [-2.0 * y[0], -2.0 * y[1], -2.0 * y[2], square, ones, ones, ones]
        a = y[0] * v[0] + y[1] * v[1] + y[2] * v[2]
        c = y[0] * n[0] + y[1] * n[1] + y[2] * n[2]
        quad = [-(v[i] * c + n[i] * a) for i in range(3)] + [a * c]
        quad += [v[i] * n[i] for i in range(3)]
        quad += [v[i] * n[j] + v[j] * n[i] for i, j in ((0, 1), (0, 2), (1, 2))]
        for values, ref in ((dist, gd_ref), (quad, gq_ref)):
            for r, value in enumerate(values):
                for p, piece in enumerate(pieces(value)):
                    put_wide(ref, (16 * p + r) * patches, piece)
        for r, value in enumerate(y + [ones]):
            for p, piece in enumerate(pieces(value)):
                if p == 0 or r < 3:
                    put_wide(gm_ref, (4 * p + r) * patches, piece)

        def one_patch(q, _):
            slot = b * patches + q
            for k in range(wtiles):
                groups = []
                for ref in (gd_ref, gq_ref):
                    h, m, l = [
                        get_tile(ref, wtiles, k, p * 16 * patches + q, 16, patches) for p in range(3)
                    ]
                    groups += [h, m, h, l, h, m]
                block = jnp.concatenate(groups, axis=0).T.astype(bf16)
                lside_ref[slot, k * LANES : (k + 1) * LANES, :] = block
            rows16 = get_wide(gm_ref, wtiles, q, 16, patches)
            lmom_ref[slot] = rows16.astype(bf16)
            return 0

        lax.fori_loop(0, patches, one_patch, 0, unroll=2)

    wall_sources(
        1, x, [wnormal_ref[i] for i in range(3)], [wdensity_ref[i] for i in range(3)], wweight_ref[...]
    )

    for copy in weights:
        copy.wait()

    def membrane(first, count):
        tiles = [strided(e_ref, first * sub + k, count, sub) for k in range(sub)]
        value = jnp.concatenate(tiles, axis=1)
        centred = (value - jnp.mean(value, axis=1, keepdims=True)).astype(bf16)
        coeff = jnp.dot(centred, analysis_ref[...], preferred_element_type=f32)
        scaled = (coeff * stiffness_ref[...]).astype(bf16)
        force = -jnp.dot(scaled, synthesis_ref[...], preferred_element_type=f32)
        for k in range(sub):
            f_ref[pl.ds(first * sub + k, count, stride=sub), :] = force[:, k * LANES : (k + 1) * LANES]

    membrane(0, 3 * rows * cols)

    def pass_on(pairs):
        for copy, row in pairs:
            copy.wait_recv()
            for onward in sideways(row):
                onward.start()
                ys.append(onward)

    all_patches = patches * size_x * size_y
    block_start = (me_x * size_y + me_y) * patches

    def put_patch(ref, t, value):
        height = ref.shape[0] // wtiles
        for k in range(wtiles):
            at = pl.multiple_of(k * height + t * value.shape[0], 8)
            ref[pl.ds(at, value.shape[0]), :] = value[:, k * LANES : (k + 1) * LANES]

    def layer_slot(t, n):
        if n == 0:
            return t + patches
        slot = pnear_ref[n - 1, t] - block_start + patches
        slot = jnp.where(slot < 0, slot + all_patches, slot)
        slot = jnp.where(slot >= all_patches, slot - all_patches, slot)
        return jnp.clip(slot, 0, 3 * patches - 1)

    def layer_pair(j, _):
        slots = [[layer_slot(2 * j + u, n) for n in range(listed + 1)] for u in range(2)]
        scalars = []
        for u in range(2):
            side = jnp.concatenate([lside_ref[slot] for slot in slots[u]], axis=0)
            both = jnp.dot(side, lfeat_ref[2 * j + u], preferred_element_type=f32)
            root = lax.rsqrt(both[:, :wpoints])
            square = root * root
            scalars.append((both[:, wpoints:] * (square * square * root)).astype(bf16))
        moment = jnp.concatenate(
            [jnp.concatenate([lmom_ref[slot] for slot in slots[u]], axis=1) for u in range(2)], axis=0
        )
        total = jnp.dot(moment, jnp.concatenate(scalars, axis=1), preferred_element_type=f32)
        for u in range(2):
            put_patch(lacc_ref, 2 * j + u, total[16 * u : 16 * u + 16, u * wpoints : (u + 1) * wpoints])
        return 0

    pass_on(xs[:1])
    for copy in ws:
        copy.wait_recv()
    for b in range(1):
        wall_sources(
            2 * b,
            [hp_ref[b, i] for i in range(3)],
            [hn_ref[b, i] for i in range(3)],
            [hd_ref[b, i] for i in range(3)],
            hw_ref[b],
        )

    pass_on(xs[1:2])
    for b in range(1, 2):
        wall_sources(
            2 * b,
            [hp_ref[b, i] for i in range(3)],
            [hn_ref[b, i] for i in range(3)],
            [hd_ref[b, i] for i in range(3)],
            hw_ref[b],
        )

    pass_on(xs[2:4])
    lax.fori_loop(0, 1, layer_pair, 0)
    pass_on(xs[4:5])
    lax.fori_loop(1, 2, layer_pair, 0)
    pass_on(xs[5:])
    lax.fori_loop(2, patches // 2, layer_pair, 0)

    for copy in ys:
        copy.wait_recv()
    membrane(3 * rows * cols, -(-3 * (shape.slots - rows * cols) // 8) * 8)

    def prepare(gids, side_ref, coef_ref, gs, gc, apart=False):
        slots = [cell_slot(shape, gid, me_x, me_y) for gid in gids]
        sources = [(cell_points(e_cells, k, shape), cell_points(f_cells, k, shape)) for k in slots]
        prepare_sources(sources, side_ref, coef_ref, gs, gc, shape, apart)

    def cell_prepare(i):
        r = lax.div(i, jnp.int32(cols))
        c = i - r * cols
        gids = [near_ref[r, n, c] for n in range(shape.near)]
        prepare(gids, cside_ref, coef_ref, gs, gc, True)

    chunks = shape.points // WIDTH
    half = shape.near * 48
    parts = []
    for n in range(shape.near):
        parts.append((None, n, slice(n * shape.points, (n + 1) * shape.points)))

    def weigh(part, cube_ref):
        return jnp.dot(coef_ref[:, part], cube_ref[part, :], preferred_element_type=f32)

    def keep(t, acc):
        for k in range(WIDTH // LANES):
            tile = t * (WIDTH // LANES) + k
            h_ref[pl.ds(tile, acc.shape[0], stride=sub), :] = acc[:, k * LANES : (k + 1) * LANES]

    def cell_sums(i):
        for t in range(chunks):
            acc = None
            for near_rows, n, part in parts:
                feat = feats_ref[i, :, t * WIDTH : (t + 1) * WIDTH]
                root = lax.rsqrt(jnp.dot(cside_ref[part, :], feat, preferred_element_type=f32))
                cubes[t % 2][part, :] = (root * root * root).astype(bf16)
                if t > 0:
                    more = weigh(part, cubes[(t - 1) % 2])
                    acc = more if acc is None else acc + more
            if t > 0:
                keep(t - 1, acc)
        acc = None
        for _, _, part in parts:
            more = weigh(part, cubes[(chunks - 1) % 2])
            acc = more if acc is None else acc + more
        keep(chunks - 1, acc)

    def cell_finish(i, best):
        r = lax.div(i, jnp.int32(cols))
        c = i - r * cols
        x = cell_points(e_cells, i, shape)

        def total(row):
            a, b, d = [h_ref[(p * COEF + row) * sub : (p * COEF + row + 1) * sub, :] for p in range(3)]
            return a + (b + d)

        parts = finish(x, total)
        own = cell_points(f_cells, i, shape)
        drag = drag_ref[r, c]
        squared = jnp.zeros_like(best)
        values = []
        for k in range(3):
            value = drag * own[k] + parts[k]
            values.append(value)
            squared = squared + value * value
        v_ref[pl.ds(pl.multiple_of(i * cell, 8), cell), :] = jnp.concatenate(values, axis=0)
        return jnp.maximum(best, squared)

    def cell_step(i, best):
        cell_sums(i)
        cell_prepare(jnp.minimum(i + 1, rows * cols - 1))
        return cell_finish(i, best)

    cell_prepare(jnp.int32(0))
    best = lax.fori_loop(0, rows * cols, cell_step, jnp.zeros((sub, LANES), f32))
    mine_ref[...] = best

    sets = ((side_ref, coef_ref, gs, gc), (side_b, coef_b, (gs_c, gs_d), (gc_c, gc_d)))

    def wall_prepare(j):
        for u in range(2):
            gids = [cpatch_ref[n, 2 * j + u] for n in range(shape.near)]
            prepare(gids, *sets[u])

    def wall_pair(j, _):
        accs, cubes2 = [], []
        for u in range(2):
            square = jnp.dot(sets[u][0][...], wfeat_ref[2 * j + u], preferred_element_type=f32)
            root = lax.rsqrt(square)
            cubes2.append((root * root * root).astype(bf16))
        for u in range(2):
            coef = sets[u][1]
            both = jnp.concatenate(
                [coef[:, n * shape.points : (n + 1) * shape.points] for n in range(shape.near)], axis=0
            )
            accs.append(jnp.dot(both, cubes2[u], preferred_element_type=f32))
        count = coef_ref.shape[0]
        for u in range(2):
            blocks = [
                accs[u][n * count : (n + 1) * count, n * wpoints : (n + 1) * wpoints]
                for n in range(shape.near)
            ]
            put_patch(wacc_ref, 2 * j + u, functools.reduce(jnp.add, blocks))
        wall_prepare(jnp.minimum(j + 1, patches // 2 - 1))
        return 0

    for r in range(rows):
        for c in range(cols):
            for i in range(3):
                at = ((r * cols + c) * 3 + i) * sub
                speed_ref[pl.ds((r * 3 + i) * sub * cols + c, sub, stride=cols), :] = v_ref[at : at + sub, :]
    wall_prepare(jnp.int32(0))
    copies = []
    for d, device in enumerate(peers_y):
        copies.append(remote(mine_ref, from_y.at[d], tsend_y.at[d], trecv_y.at[d], device))
        copies[-1].start()
    lax.fori_loop(0, 1, wall_pair, 0)
    speeds = pltpu.make_async_copy(speed_ref, speed_hbm, local.at[8])
    speeds.start()
    best = mine_ref[...]
    for d, copy in enumerate(copies):
        copy.wait_recv()
        best = jnp.maximum(best, from_y[d])
    row_ref[...] = best
    moment = [get_wide(lacc_ref, wtiles, r, patches, 16) for r in range(11)]
    moment = [moment[i] + (moment[4 + i] + moment[8 + i]) for i in range(3)] + [moment[3]]
    for i in range(3):
        half_ref[i] = x[i] * moment[3] - moment[i]
    for d, device in enumerate(peers_x):
        copies.append(remote(row_ref, from_x.at[d], tsend_x.at[d], trecv_x.at[d], device))
        copies[-1].start()
    lax.fori_loop(1, patches // 2, wall_pair, 0)

    def wall_total(row):
        a, b, d = [
            get_wide(wacc_ref, wtiles, p * COEF + row, patches, coef_ref.shape[0]) for p in range(3)
        ]
        return a + (b + d)

    flow = finish(x, wall_total)
    for i in range(3):
        half_ref[i] = half_ref[i] + flow[i]

    best = row_ref[...]
    for d, copy in enumerate(copies[size_y - 1 :]):
        copy.wait_recv()
        best = jnp.maximum(best, from_x[d])
    top_ref[...] = best
    speeds.wait()
    for copy, _ in xs:
        copy.wait_send()
    for copy in ws + ys + copies:
        copy.wait_send()


def update_kernel(pos_ref, speed_ref, top_ref, half_ref, moved_ref, dens_ref):
    top = jnp.sqrt(jnp.max(top_ref[...], keepdims=True))
    step = 1.0 / (top + 1e-06)
    moved_ref[...] = pos_ref[...] + step * speed_ref[...]
    dens_ref[...] = 2.0 * half_ref[...]


def body(
    cell_pos,
    cell_drag,
    cell_near,
    analysis,
    stiffness,
    synthesis,
    wall_pos,
    wall_normal,
    wall_weight,
    density,
    patch_near,
    cell_to_patch,
):
    rows, cols, _, points = cell_pos.shape
    size_x, size_y = lax.axis_size("cx"), lax.axis_size("cy")
    near = cell_near.shape[2]
    listed = patch_near.shape[1]
    patches, _, wpoints = wall_pos.shape
    shape = Shape(rows, cols, points, size_x, size_y, near)
    sub, cell = shape.sub, shape.cell
    raw = cell_pos.reshape(rows, cols, 3, sub, LANES)
    raw = jnp.transpose(raw, (0, 2, 3, 1, 4)).reshape(rows * 3 * sub * cols, LANES)
    wtiles = wpoints // LANES
    spare = -(-shape.slots // 8) * 8
    sources = near * points
    assert cell_to_patch.shape[1] == near and patches % 2 == 0
    coef_rows = -(-3 * COEF // 16) * 16
    dma = pltpu.SemaphoreType.DMA
    vmem = pltpu.VMEM
    in_vmem = pl.BlockSpec(memory_space=pltpu.VMEM)
    in_smem = pl.BlockSpec(memory_space=pltpu.SMEM)
    in_hbm = pl.BlockSpec(memory_space=pltpu.HBM)
    walls = lambda v: jnp.transpose(v, (1, 0, 2))
    speed, top, half = pl.pallas_call(
        functools.partial(mega_kernel, shape, listed),
        out_shape=(
            jax.ShapeDtypeStruct(raw.shape, f32),
            jax.ShapeDtypeStruct((sub, LANES), f32),
            jax.ShapeDtypeStruct((3, patches, wpoints), f32),
        ),
        in_specs=[
            in_smem, in_smem, in_hbm, in_hbm, in_hbm, in_hbm,
            in_hbm, in_hbm, in_hbm, in_hbm, in_smem, in_smem,
        ],
        out_specs=[in_hbm, in_vmem, in_vmem],
        scratch_shapes=[
            vmem(raw.shape, f32),
            vmem(raw.shape, f32),
            vmem((1, stiffness.shape[0]), f32),
            vmem((3, patches, wpoints), f32),
            vmem((3, patches, wpoints), f32),
            vmem((patches, wpoints), f32),
            vmem((3, patches, wpoints), f32),
            vmem(analysis.shape, bf16),
            vmem(synthesis.shape, bf16),
            vmem((spare, cell, LANES), f32),
            vmem((spare, cell, LANES), f32),
            vmem((rows * cols * cell, LANES), f32),
            vmem((24 * sub, LANES), f32),
            vmem((24 * sub, LANES), f32),
            vmem((24 * sub, LANES), f32),
            vmem((24 * sub, LANES), f32),
            vmem((coef_rows * sub, LANES), f32),
            vmem((coef_rows * sub, LANES), f32),
            vmem((coef_rows * sub, LANES), f32),
            vmem((coef_rows * sub, LANES), f32),
            vmem((24 * sub, LANES), f32),
            vmem((points, near * 48), bf16),
            vmem((sources, 48), bf16),
            vmem((coef_rows, sources), bf16),
            vmem((points, near * 48), bf16),
            vmem((coef_rows, sources), bf16),
            vmem((rows * cols, 48, points), bf16),
            vmem((sources, WIDTH), bf16),
            vmem((sources, WIDTH), bf16),
            vmem((coef_rows * sub, LANES), f32),
            vmem((2, 3, patches, wpoints), f32),
            vmem((2, 3, patches, wpoints), f32),
            vmem((2, 3, patches, wpoints), f32),
            vmem((2, patches, wpoints), f32),
            vmem((48 * patches * wtiles, LANES), f32),
            vmem((48 * patches * wtiles, LANES), f32),
            vmem((16 * patches * wtiles, LANES), f32),
            vmem((48 * patches * wtiles, LANES), f32),
            vmem((24 * patches * wtiles, LANES), f32),
            vmem((3 * patches, wpoints, 192), bf16),
            vmem((3 * patches, 16, wpoints), bf16),
            vmem((patches, 192, 2 * wpoints), bf16),
            vmem((patches, near * 48, near * wpoints), bf16),
            vmem((patches * 16 * wtiles, LANES), f32),
            vmem((patches * coef_rows * wtiles, LANES), f32),
            vmem((sub, LANES), f32),
            vmem((sub, LANES), f32),
            vmem((size_y - 1, sub, LANES), f32),
            vmem((size_x - 1, sub, LANES), f32),
            dma((9,)),
            dma((2 * HALO,)),
            dma((2 * HALO,)),
            dma((2 * shape.ext_rows,)),
            dma((2 * shape.ext_rows,)),
            dma((8,)),
            dma((8,)),
            dma((size_y - 1,)),
            dma((size_y - 1,)),
            dma((size_x - 1,)),
            dma((size_x - 1,)),
        ],
        compiler_params=pltpu.CompilerParams(
            collective_id=0, has_side_effects=True, vmem_limit_bytes=62 * 2**20
        ),
        name="mega",
    )(
        jnp.transpose(cell_near, (0, 2, 1)),
        cell_drag,
        raw,
        analysis,
        stiffness[None, :],
        synthesis,
        walls(wall_pos),
        walls(wall_normal),
        wall_weight,
        walls(density),
        jnp.transpose(patch_near),
        jnp.transpose(cell_to_patch),
    )
    moved, dens = pl.pallas_call(
        update_kernel,
        out_shape=(
            jax.ShapeDtypeStruct(raw.shape, f32),
            jax.ShapeDtypeStruct((3, patches, wpoints), f32),
        ),
        in_specs=[in_vmem] * 4,
        out_specs=[in_vmem] * 2,
        name="update",
    )(raw, speed, top, half)
    moved = jnp.transpose(moved.reshape(rows, 3, sub, cols, LANES), (0, 3, 1, 2, 4))
    return moved.reshape(cell_pos.shape), jnp.transpose(dens, (1, 0, 2))


def solution(mesh):
    placed = (
        P("cx", "cy", None, None),
        P("cx", "cy"),
        P("cx", "cy", None),
        P(),
        P(),
        P(),
        P(("cx", "cy"), None, None),
        P(("cx", "cy"), None, None),
        P(("cx", "cy"), None),
        P(("cx", "cy"), None, None),
        P(("cx", "cy"), None),
        P(("cx", "cy"), None),
    )
    return jax.shard_map(
        body,
        mesh=mesh,
        in_specs=placed,
        out_specs=(P("cx", "cy", None, None), P(("cx", "cy"), None, None)),
        check_vma=False,
    )
```
